128 devices in a mesh: grp: 4 (over z_lo, core), tile: 32 (over x, y, z_hi).
Axes of the slice: x: 4, y: 4, z: 4 (z_hi: 2, z_lo: 2; z = z_hi * 2 + z_lo), core: 2. Of those that a mesh axis runs over, the one named last changes fastest.
Arguments:
- start_velocity: float32 [2, 128, 16384], P(None, 'grp', 'tile'), may hold values from -6 to 6
- driving_stress: float32 [2, 128, 16384], P(None, 'grp', 'tile'), may hold values from -6 to 6
- viscosity: float32 [2, 128, 16384], P(None, 'grp', 'tile'), may hold values from 0.3 to 3
- friction: float32 [128, 16384], P('grp', 'tile'), may hold values from 0.02 to 0.5
- cell_element: int32 [128, 16384], P('grp', 'tile'), may hold values from 0 to 16383, as said below
- observed: float32 [65536, 256], P(('grp', 'tile')), may hold values from -6 to 6
- look: float32 [2, 65536, 256], P(None, ('grp', 'tile')), may hold values from -3 to 3
- row_owner: int32 [65536, 1], P(('grp', 'tile')), may hold values from 0 to 127; in each aligned block of 512 rows (0 to 511, 512 to 1023, ...) at most 8 rows name the same one
- row_cell: int32 [65536], P(('grp', 'tile')), may hold values from 0 to 16383
Outputs:
- stress_adjoint: float32 [2, 128, 16384], P(None, 'grp', 'tile')
- friction_adjoint: float32 [16384], P(('grp', 'tile'))
The draws below stay inside these ranges and needn't reach their ends.
Inputs may be any that keep to these rules, and one draw needn't show every extreme that they name: `row_owner`: of the 512 rows of one device at most 8 name the same owner, and in some blocks one owner is named by exactly 8 rows. `cell_element`: the element of a node held by the device with grp index g lies in g * 128 * 32 to (g + 1) * 128 * 32 - 1; element e is owned by the device at flattened index e // 128.
All inputs are finite; a program needn't handle non-finite values.
Results may differ from the reference program's by a relative error of at most 0.00002.
Values sent between devices are 32-bit elements; how exact they have to be, the bound alone decides.
A program may use at most 128 MiB of HBM per device.

```python
import math
import jax
import jax.numpy as jnp
import numpy as np

CX = 32
CY = 512
R_DEV = 512
EPOCHS = 256
SWEEPS = 8
PICARD = 2
NX = 128
NY = 16384
ROWS = 65536
CAP = 8
ELEMENTS = 16384
N_TILE = 32
DEVICES = 128


def draw_cell_element(key, part):
    group_width = CX * NY // 128
    rows_i = jnp.arange(NX, dtype=jnp.int32)[:, None]
    within = jax.random.randint(key, (NX, NY), 0, group_width)
    return (rows_i // CX * group_width + within).astype(jnp.int32)


def with_ends(values, rng, low, largest):
    longest = values.shape.index(max(values.shape))
    spots = []
    for shift in (0, 1):
        where = [jax.random.randint(jax.random.fold_in(rng, axis), (), 0, length) for axis, length in enumerate(values.shape)]
        where[longest] = (where[longest] + shift) % values.shape[longest]
        spots.append(tuple(where))
    return values.at[spots[0]].set(low).at[spots[1]].set(largest)


def steps_of(key, extent, cuts, low, high):
    factor_of = 1.0
    for position, shards_of in cuts:
        draws = jax.random.uniform(jax.random.fold_in(jax.random.fold_in(key, 6), position), (shards_of,), jnp.float32, low / len(cuts), high / len(cuts))
        factor_of = factor_of * jnp.repeat(jnp.exp(draws), extent[position] // shards_of).reshape((-1,) + (1,) * (len(extent) - 1 - position))
    return factor_of


def assign_block(stream_key, own, number, rows, number_of, top, reach, skew):
    order = jax.random.permutation(stream_key, number_of)
    crowded, ordinary = portions_of(number_of, rows * top, reach, skew, True), portions_of(number_of, rows * top, reach, skew, False)
    places = jnp.arange(number_of)

    def named(tallies, rotation):
        used = int((tallies > 0).sum())
        fixed = max(1, used // 4)
        moved = fixed + (places - fixed + rotation * (used - fixed)) % max(1, number_of - fixed)
        return jnp.zeros((number_of,), jnp.int32).at[order[jnp.where(places < fixed, places, moved)]].set(jnp.asarray(tallies, jnp.int32))

    tallies = jnp.where(number % 4 == 0, named(crowded, number // 4), named(ordinary, number - number // 4 - 1))
    mixed = jax.random.permutation(jax.random.fold_in(own, 3), number_of)
    giver, taker = mixed[0:number_of // 2 * 2:2], mixed[1:number_of // 2 * 2:2]
    margin = jnp.minimum(tallies[giver] - 1, reach - tallies[taker]) // 2
    margin = jnp.where((giver == order[0]) | (taker == order[0]) | (tallies[taker] == 0), 0, jnp.maximum(margin, 0))
    moved = jax.random.randint(jax.random.fold_in(own, 4), (number_of // 2,), 0, 1 << 20) % (margin + 1)
    tallies = tallies.at[giver].add(-moved).at[taker].add(moved)
    members = jnp.searchsorted(jnp.cumsum(tallies), jnp.arange(rows * top), side="right").astype(jnp.int32)
    grid = members.reshape(top, rows).T
    grid = grid[jax.random.permutation(jax.random.fold_in(own, 1), rows)]
    rotation = jax.random.randint(jax.random.fold_in(own, 2), (rows, 1), 0, top)
    return jnp.take_along_axis(grid, (jnp.arange(top)[None, :] + rotation) % top, axis=1)


def portions_of(amount, total, limit, skew, full):
    weights = [(1 << 20) // math.isqrt(rank ** skew) + 1 for rank in range(1, amount + 1)]
    largest = limit if full else min(limit, max(-(-total // amount), total * weights[0] // sum(weights)))
    least = 1 if total - largest >= amount - 1 else 0
    given, surplus = [largest] + [least] * (amount - 1), total - largest - least * (amount - 1)
    while surplus > 0:
        candidates = [i for i in range(1, amount) if given[i] < largest] or [i for i in range(1, amount) if given[i] < limit]
        whole, left = sum([weights[i] for i in candidates]), surplus
        for i in candidates:
            addition = min(limit - given[i], max(1, left * weights[i] // whole), surplus)
            given[i] = given[i] + addition
            surplus = surplus - addition
    return np.array(given)


def gaussian(stream_key, dims, width, bound, shards=(), held_as=jnp.bfloat16):
    values = width * jax.random.normal(stream_key, dims, jnp.float32)
    if shards:
        values = values * steps_of(stream_key, dims, shards, -0.22, 0.18)
    return jnp.clip(values, -bound, bound).astype(held_as)


def setup_inputs(seed: int = 0) -> dict:
    key_of = jax.random.split(jax.random.key(seed), 10)
    start_velocity = gaussian(key_of[0], (2, NX, NY), 1.0, 6.0, ((1, 4), (2, 32)), jnp.float32)
    driving_stress = gaussian(key_of[1], (2, NX, NY), 1.0, 6.0, ((1, 4), (2, 32)), jnp.float32)
    viscosity = jnp.clip(jnp.exp(math.log(3.0) - 2.3025851 * jax.random.uniform(key_of[2], (PICARD, NX, NY), jnp.float32) ** steps_of(key_of[2], (PICARD, NX, NY), ((1, 4), (2, 32)), -0.2, 0.2)), 0.3, 3.0)
    friction = jnp.clip(jnp.exp(math.log(0.5) - 3.218876 * jax.random.uniform(key_of[3], (NX, NY), jnp.float32) ** steps_of(key_of[3], (NX, NY), ((0, 4), (1, 32)), -0.2, 0.2)), 0.02, 0.5)
    cell_element = draw_cell_element(jax.random.fold_in(key_of[9], 71), 0)
    observed = gaussian(key_of[5], (ROWS, EPOCHS), 1.0, 6.0, ((0, 128),), jnp.float32)
    look = gaussian(key_of[6], (2, ROWS, EPOCHS), 0.5, 3.0, ((1, 128),), jnp.float32)
    row_owner_keys = jax.random.split(jax.random.fold_in(key_of[7], 1), ROWS // R_DEV)
    row_owner_turns = jax.random.permutation(jax.random.fold_in(key_of[7], 3), ROWS // R_DEV)
    row_owner = jax.vmap(lambda own, number: assign_block(jax.random.fold_in(key_of[7], 2), own, number, R_DEV, DEVICES, 1, CAP, 2))(row_owner_keys, row_owner_turns).reshape((ROWS, 1))
    row_cell = with_ends(jax.random.randint(key_of[8], (ROWS,), 0, CX * CY), jax.random.fold_in(key_of[8], 1), 0, (CX * CY) - 1).astype(jnp.int32)
    return {"start_velocity": start_velocity, "driving_stress": driving_stress, "viscosity": viscosity, "friction": friction, "cell_element": cell_element, "observed": observed, "look": look, "row_owner": row_owner, "row_cell": row_cell}


def grad_x(p):
    return 0.5 * (p[1:, 1:] + p[1:, :-1] - p[:-1, 1:] - p[:-1, :-1])

def grad_y(p):
    return 0.5 * (p[1:, 1:] + p[:-1, 1:] - p[1:, :-1] - p[:-1, :-1])

def spread_x(t):
    return 0.5 * (t[:-1, :-1] + t[:-1, 1:] - t[1:, :-1] - t[1:, 1:])

def spread_y(t):
    return 0.5 * (t[:-1, :-1] + t[1:, :-1] - t[:-1, 1:] - t[1:, 1:])

def corner_mean(e):
    return 0.25 * (e[1:, 1:] + e[1:, :-1] + e[:-1, 1:] + e[:-1, :-1])

def operate(padded, quad_visc, friction_eff):
    values = padded[:, 1:-1, 1:-1]
    u_dx = grad_x(padded[0])
    u_dy = grad_y(padded[0])
    v_dx = grad_x(padded[1])
    v_dy = grad_y(padded[1])
    stress_xx = quad_visc * (4.0 * u_dx + 2.0 * v_dy)
    stress_yy = quad_visc * (4.0 * v_dy + 2.0 * u_dx)
    stress_xy = quad_visc * (u_dy + v_dx)
    first = spread_x(stress_xx) + spread_y(stress_xy) + friction_eff * values[0]
    second = spread_y(stress_yy) + spread_x(stress_xy) + friction_eff * values[1]
    return jnp.stack([first, second])

def one_sweep(velocity, quad_visc, friction_eff, precond, stress):
    padded = jnp.pad(velocity, ((0, 0), (1, 1), (1, 1)))
    return velocity + precond * (stress - operate(padded, quad_visc, friction_eff))

def reference(start_velocity, driving_stress, viscosity, friction, cell_element, observed, look, row_owner, row_cell):
    padded_visc = jnp.pad(viscosity, ((0, 0), (1, 1), (1, 1)))
    quad_list = [corner_mean(padded_visc[picard]) for picard in range(PICARD)]
    owner_dev = row_owner[:, 0].astype(jnp.int32)
    cell_index = (owner_dev // N_TILE * CX + row_cell // CY) * NY + owner_dev % N_TILE * CY + row_cell % CY
    sweep_fn = jax.checkpoint(one_sweep)

    def misfit(stress, log_factor):
        friction_eff = friction * jnp.exp(log_factor[cell_element])
        velocity = start_velocity
        for picard in range(PICARD):
            quad_visc = quad_list[picard]
            diagonal = 1.25 * (quad_visc[:-1, :-1] + quad_visc[:-1, 1:] + quad_visc[1:, :-1] + quad_visc[1:, 1:]) + friction_eff
            precond = 0.45 / diagonal
            for _ in range(SWEEPS):
                velocity = sweep_fn(velocity, quad_visc, friction_eff, precond, stress)
        speeds = velocity.reshape(2, NX * NY)[:, cell_index]
        misfit_rows = look[0] * speeds[0][:, None] + look[1] * speeds[1][:, None] - observed
        return 0.5 * jnp.sum(misfit_rows * misfit_rows) / math.sqrt(EPOCHS)
    value, pullback = jax.vjp(misfit, driving_stress, jnp.zeros((ELEMENTS,), jnp.float32))
    stress_adjoint, friction_adjoint = pullback(jnp.ones_like(value))
    return (stress_adjoint, friction_adjoint)
```

```python
import functools

import jax
import jax.numpy as jnp
from jax import lax
from jax.experimental import pallas as pl
from jax.experimental.pallas import tpu as pltpu
from jax.sharding import PartitionSpec as P

MESH = pl.DeviceIdType.MESH
CX, CY = 32, 512
SWEEPS, PICARD = 8, 2
STEPS = SWEEPS * PICARD
W = 16
EX = CX + 2 * W
SEG = 8
LANES = 128
NF = 7
SLOTS = 8
F32, BF16, I32 = jnp.float32, jnp.bfloat16, jnp.int32
FORWARD = ((0, 4), (4, 4), (8, 4), (12, 4))
BACKWARD = ((0, 4), (4, 4), (8, 4), (12, 3))


def roll(x, amount):
    return pltpu.roll(x, amount % LANES, 1)


def right(x):
    return roll(x, -1)


def left(x):
    return roll(x, 1)


def pieces(x):
    high = x.astype(BF16)
    rest = x - high.astype(F32)
    middle = rest.astype(BF16)
    return high, middle, (rest - middle.astype(F32)).astype(BF16)


def iota(shape, dim):
    return lax.broadcasted_iota(I32, shape, dim)


def rows_kernel(n_grp, n_tile, look, observed, owner, cell, out):
    rows, epochs = observed.shape
    devices = n_grp * n_tile
    owner_row = owner[...]
    lane = iota((rows, LANES), 1)
    owner_col = jnp.transpose(jnp.broadcast_to(owner_row.astype(F32), (LANES, rows)))
    cell_col = jnp.transpose(jnp.broadcast_to(cell[...].astype(F32), (LANES, rows)))
    mark = owner_col == lane.astype(F32)
    marks = jnp.where(mark, 1.0, 0.0)
    below = jnp.where(iota((rows, rows), 0) > iota((rows, rows), 1), 1.0, 0.0).astype(BF16)
    before = jnp.dot(below, marks.astype(BF16), preferred_element_type=F32)
    rank = jnp.sum(before * marks, axis=1, keepdims=True)
    x, y, o = look[0], look[1], observed[...]
    sums = [jnp.sum(a * b, axis=1, keepdims=True) for a, b in ((x, x), (x, y), (y, y), (x, o), (y, o))]
    value = cell_col
    for j, part in enumerate(sums):
        value = jnp.where(lane >= SLOTS * (j + 1), part, value)
    keep = (rank == (lane % SLOTS).astype(F32)) & (lane < SLOTS * 6)
    value = jnp.where(keep, value, 0.0)
    place = owner_row % n_tile * 8 + owner_row // n_tile
    chosen = jnp.where(iota((n_tile * 8, rows), 0) == place, 1.0, 0.0).astype(BF16)
    total = sum(jnp.dot(chosen, piece, preferred_element_type=F32) for piece in pieces(value))
    out[...] = total.reshape(n_tile, 8, LANES)


def main_kernel(
    n_grp, n_tile,
    vel, stress, visc, fric, elem, outgoing,
    stress_out, elem_out,
    edge_l, edge_r, halo_t, halo_b, halo_l, halo_r,
    adj_n, adj_t, adj_b, aedge_l, aedge_r, ahalo_l, ahalo_r,
    first_r, second_s, second_r, gram_a, gram_b, gram,
    fields, half_q, quart_q, prec, keep_c, drive_u, drive_v,
    moments, adj, grads, grad_n, one_lo, elem_s, elem_r,
    send_sem, recv_sem, asend_sem, arecv_sem, row_send, row_recv, grp_send, grp_recv, el_send, el_recv,
):
    g, t = lax.axis_index("grp"), lax.axis_index("tile")
    fields2 = fields.reshape(NF * EX * SEG, LANES)
    lane8 = iota((8, LANES), 1)

    barrier = pltpu.get_barrier_semaphore()
    for ref in (halo_t, halo_b, halo_l, halo_r, adj_t, adj_b, ahalo_l, ahalo_r):
        ref[...] = jnp.zeros_like(ref)

    def greet(device):
        pl.semaphore_signal(barrier, inc=1, device_id=device, device_id_type=MESH)

    up, down, west, east = g > 0, g < n_grp - 1, t > 0, t < n_tile - 1
    for step in range(1, n_grp):
        greet((lax.rem(g + step, n_grp), t))

    def greet_tile(step, carry):
        greet((g, lax.rem(t + step, n_tile)))
        return carry

    lax.fori_loop(1, n_tile, greet_tile, 0)
    diagonals = ((up & west, -1, -1), (up & east, -1, 1), (down & west, 1, -1), (down & east, 1, 1))
    total = n_grp - 1 + n_tile - 1
    for there, dg, dt in diagonals:
        pl.when(there)(functools.partial(greet, (g + dg, t + dt)))
        total = total + there.astype(I32)

    natural = [(vel, 0), (vel, 1), (stress, 0), (stress, 1), (visc, 0), (visc, 1), (fric, None)]

    def tile_of(f, r, m):
        ref, index = natural[f]
        where = (pl.ds(8 * r, 8), pl.ds(LANES * m, LANES))
        return ref[where] if index is None else ref[(index,) + where]

    for r in range(CX // 8):
        low, high = None, None
        for f in range(NF):
            a = roll(tile_of(f, r, 0), 16 * f)
            b = roll(tile_of(f, r, CY // LANES - 1), 16 * f + 16)
            low = a if low is None else jnp.where(lane8 >= 16 * f, a, low)
            high = b if high is None else jnp.where(lane8 >= 16 * f, b, high)
        edge_l[pl.ds(8 * r, 8), :] = low
        edge_r[pl.ds(8 * r, 8), :] = high

    pl.semaphore_wait(barrier, total)

    def neighbours(blocks, e_l, e_r, h_l, h_r, send, recv):
        moves = []
        for ref, h_t, h_b in blocks:
            moves.append((down, up, ref(W), h_t, (g + 1, t)))
            moves.append((up, down, ref(0), h_b, (g - 1, t)))
        moves.append((east, west, e_r, h_l.at[pl.ds(W, CX)], (g, t + 1)))
        moves.append((west, east, e_l, h_r.at[pl.ds(W, CX)], (g, t - 1)))
        last, head, foot = pl.ds(W, W), pl.ds(0, W), pl.ds(W + CX, W)
        moves.append((down & east, up & west, e_r.at[last], h_l.at[head], (g + 1, t + 1)))
        moves.append((up & east, down & west, e_r.at[head], h_l.at[foot], (g - 1, t + 1)))
        moves.append((down & west, up & east, e_l.at[last], h_r.at[head], (g + 1, t - 1)))
        moves.append((up & west, down & east, e_l.at[head], h_r.at[foot], (g - 1, t - 1)))
        out = []
        for i, (sends, gets, source, target, device) in enumerate(moves):
            copy = pltpu.make_async_remote_copy(
                src_ref=source, dst_ref=target, send_sem=send.at[i], recv_sem=recv.at[i],
                device_id=device, device_id_type=MESH,
            )
            out.append((sends, gets, copy))
        return out

    def begin(moves):
        for sends, _, copy in moves:
            pl.when(sends)(copy.start)

    def arrive(moves):
        for _, gets, copy in moves:
            pl.when(gets)(copy.wait_recv)

    def leave(moves):
        for sends, _, copy in moves:
            pl.when(sends)(copy.wait_send)

    def rows_of(ref):
        if len(ref.shape) == 2:
            return lambda start: ref.at[pl.ds(start, W), :]
        return lambda start: ref.at[:, pl.ds(start, W), :]

    moves = neighbours(
        [
            (rows_of(vel), halo_t.at[pl.ds(0, 2)], halo_b.at[pl.ds(0, 2)]),
            (rows_of(stress), halo_t.at[pl.ds(2, 2)], halo_b.at[pl.ds(2, 2)]),
            (rows_of(visc), halo_t.at[pl.ds(4, 2)], halo_b.at[pl.ds(4, 2)]),
            (rows_of(fric), halo_t.at[6], halo_b.at[6]),
        ],
        edge_l, edge_r, halo_l, halo_r, send_sem, recv_sem,
    )
    begin(moves)

    def send_rows(step, carry):
        to = lax.rem(t + step, n_tile)
        pltpu.make_async_remote_copy(
            src_ref=outgoing.at[to], dst_ref=first_r.at[t], send_sem=row_send, recv_sem=row_recv,
            device_id=(g, to), device_id_type=MESH,
        ).start()
        return carry

    lax.fori_loop(1, n_tile, send_rows, 0)

    first_element = g * (n_tile * LANES)
    for r in range(CX):
        low = (elem[pl.ds(r, 1), :] - first_element) % LANES
        one_lo[r] = jnp.where(iota((LANES, CY), 0) == low, 1.0, 0.0).astype(BF16)

    def spread(target, base, row, tiles, before, after):
        wide = [roll(x, 32) for x in tiles]
        back = [roll(x, -32) for x in tiles]
        for m in range(CY // LANES):
            even = jnp.where(lane8 < 32, before if m == 0 else wide[m - 1], wide[m])
            odd = jnp.where(lane8 < 96, back[m], after if m == CY // LANES - 1 else back[m + 1])
            target[pl.ds((base + row) * SEG + 2 * m, 8, stride=SEG), :] = even
            target[pl.ds((base + row) * SEG + 2 * m + 1, 8, stride=SEG), :] = odd

    def spread_block(f, r, tiles):
        at = pl.ds(8 * r, 8)
        spread(
            fields2, f * EX, 8 * r, tiles,
            roll(halo_l[at, :], 16 - 16 * f), roll(halo_r[at, :], 96 - 16 * f),
        )

    arrive(moves)
    for f in range(NF):
        for r in range(EX // 8):
            if r < W // 8:
                tiles = [halo_t[f, pl.ds(8 * r, 8), pl.ds(LANES * m, LANES)] for m in range(4)]
            elif r >= (W + CX) // 8:
                k = r - (W + CX) // 8
                tiles = [halo_b[f, pl.ds(8 * k, 8), pl.ds(LANES * m, LANES)] for m in range(4)]
            else:
                tiles = [tile_of(f, r - W // 8, m) for m in range(4)]
            spread_block(f, r, tiles)

    seg8 = iota((SEG, LANES), 0)
    inside = ((t > 0) | (seg8 > 0) | (lane8 >= 32)) & ((t < n_tile - 1) | (seg8 < SEG - 1) | (lane8 < 96))
    inside_top = inside & up
    inside_bottom = inside & down
    for p in range(PICARD):
        pair = fields[4 + p, 0]
        pair = pair + right(pair)
        q_old = None
        for k in range(EX - 1):
            other = fields[4 + p, k + 1]
            other = other + right(other)
            q = 0.25 * (pair + other)
            pair = other
            half_q[p, k] = 0.5 * q
            quart_q[p, k] = 0.25 * q
            if q_old is not None:
                both = q_old + q
                b = fields[6, k]
                diagonal = 1.25 * (both + left(both)) + b
                mask = inside_top if k < W else inside_bottom if k >= W + CX else inside
                c = jnp.where(mask, 0.45 / diagonal, 0.0)
                prec[p, k] = c
                keep_c[p, k] = jnp.where(mask, 1.0 - c * b, 0.0)
                drive_u[p, k] = c * fields[2, k]
                drive_v[p, k] = c * fields[3, k]
            q_old = q

    def stencil(load, p, lo, hi, use):
        prev, stress_prev = None, None
        for k in range(lo - 1, hi + 2):
            a, b = load(k)
            la, lb = right(a), right(b)
            xa, yb = a + la, lb - b
            ya, xb = la - a, b + lb
            plus, minus = ya + xb, ya - xb
            now = None
            if prev is not None:
                xm = xa - prev[0]
                ym = yb + prev[1]
                sh = plus + prev[2]
                both = xm + ym
                h = half_q[p, k - 1]
                now = (h * (both + xm), h * (both + ym), quart_q[p, k - 1] * sh)
                if stress_prev is not None:
                    dxx = stress_prev[0] - now[0]
                    myy = stress_prev[1] + now[1]
                    mxy = stress_prev[2] + now[2]
                    dxy = stress_prev[2] - now[2]
                    use(k - 1, (dxx - mxy) + left(dxx + mxy), (dxy - myy) + left(dxy + myy), prev[3], prev[4])
            prev, stress_prev = (xa, yb, minus, a, b), now

    inv = 1.0 / 0.45

    def forward(start, count):
        p = start // SWEEPS
        lo, hi = start + 1, EX - 2 - start

        def sweep(s, carry):
            def use(k, first, second, u, v):
                c, d = prec[p, k], keep_c[p, k]
                new_u = (d * u + drive_u[p, k]) - c * first
                new_v = (d * v + drive_v[p, k]) - c * second
                fields[0, k] = new_u
                fields[1, k] = new_v
                if W <= k < W + CX:
                    moments[s, 0, k - W] = inv * new_u + (1.0 - inv) * u
                    moments[s, 1, k - W] = inv * new_v + (1.0 - inv) * v

            stencil(lambda k: (fields[0, k], fields[1, k]), p, lo, hi, use)
            return carry

        lax.fori_loop(start, start + count, sweep, 0)

    for start, count in FORWARD[:2]:
        forward(start, count)

    everyone = pl.ds(0, n_tile - 1)
    pltpu.make_async_remote_copy(
        src_ref=outgoing.at[everyone], dst_ref=first_r.at[everyone], send_sem=row_send, recv_sem=row_recv,
        device_id=(g, t), device_id_type=MESH,
    ).wait()
    own = outgoing[t]
    first_r[t] = own
    flat_r = first_r.reshape(n_tile * 8, LANES)
    for k in range(n_grp):
        second_s[k] = flat_r[pl.ds(k, n_tile, stride=8), :]
    second_r[g] = second_s[g]

    def group_copy(step):
        to = lax.rem(g + step, n_grp)
        return pltpu.make_async_remote_copy(
            src_ref=second_s.at[to], dst_ref=second_r.at[g], send_sem=grp_send.at[step - 1],
            recv_sem=grp_recv.at[step - 1], device_id=(to, t), device_id_type=MESH,
        )

    for step in range(1, n_grp):
        group_copy(step).start()

    forward(*FORWARD[2])

    for step in range(1, n_grp):
        group_copy(step).wait()
    sources = n_grp * n_tile
    arrived = jnp.transpose(second_r[...].reshape(sources, LANES))
    for s in range(SLOTS):
        cell = arrived[s : s + 1, :].astype(I32)
        at = pl.ds(s * sources, sources)
        gram_b[:, at] = jnp.where(iota((CY, sources), 0) == cell % CY, 1.0, 0.0).astype(BF16)
        chosen = iota((CX, sources), 0) == cell // CY
        for j in range(5):
            row = SLOTS * (j + 1) + s
            value = jnp.where(chosen, arrived[row : row + 1, :], 0.0)
            for q, piece in enumerate(pieces(value)):
                gram_a[pl.ds((q * 5 + j) * CX, CX), at] = piece
    product = lax.dot_general(
        gram_a[...], gram_b[...], (((1,), (1,)), ((), ())), preferred_element_type=F32
    )
    part = 5 * CX
    gram[...] = product[:part] + product[part : 2 * part] + product[2 * part :]

    forward(*FORWARD[3])

    def collect(source, base, r, m):
        a = source[pl.ds(base * SEG + 8 * SEG * r + 2 * m, 8, stride=SEG), :]
        b = source[pl.ds(base * SEG + 8 * SEG * r + 2 * m + 1, 8, stride=SEG), :]
        return jnp.where(lane8 < 64, roll(a, -32), roll(b, 32))

    scale = 1.0 / 16.0
    for r in range(CX // 8):
        for m in range(CY // LANES):
            u = collect(fields2, W, r, m)
            v = collect(fields2, EX + W, r, m)
            at = pl.ds(LANES * m, LANES)
            sxx, sxy, syy, sxo, syo = [gram[pl.ds(j * CX + 8 * r, 8), at] for j in range(5)]
            adj_n[0, pl.ds(8 * r, 8), at] = scale * (sxx * u + sxy * v - sxo)
            adj_n[1, pl.ds(8 * r, 8), at] = scale * (sxy * u + syy * v - syo)
        rows = pl.ds(8 * r, 8)
        aedge_l[rows, :] = jnp.where(
            lane8 < 16, adj_n[0, rows, pl.ds(0, LANES)], roll(adj_n[1, rows, pl.ds(0, LANES)], 16)
        )
        end = pl.ds(CY - LANES, LANES)
        aedge_r[rows, :] = jnp.where(
            lane8 < 16, roll(adj_n[0, rows, end], 16), roll(adj_n[1, rows, end], 32)
        )
    amoves = neighbours(
        [(rows_of(adj_n), adj_t, adj_b)], aedge_l, aedge_r, ahalo_l, ahalo_r, asend_sem, arecv_sem
    )
    begin(amoves)
    grads[...] = jnp.zeros_like(grads)
    arrive(amoves)
    adj2 = adj.reshape(2 * EX * SEG, LANES)
    for f in range(2):
        for r in range(EX // 8):
            if r < W // 8:
                source, k = adj_t, r
            elif r >= (W + CX) // 8:
                source, k = adj_b, r - (W + CX) // 8
            else:
                source, k = adj_n, r - W // 8
            tiles = [source[f, pl.ds(8 * k, 8), pl.ds(LANES * m, LANES)] for m in range(4)]
            at = pl.ds(8 * r, 8)
            spread(
                adj2, f * EX, 8 * r, tiles,
                roll(ahalo_l[at, :], 16 - 16 * f), roll(ahalo_r[at, :], 96 - 16 * f),
            )

    def gather(position, k, a, b):
        i = k - W
        grads[0, i] = grads[0, i] + a
        grads[1, i] = grads[1, i] + b
        grads[2, i] = grads[2, i] - (a * moments[position, 0, i] + b * moments[position, 1, i])

    def backward(start, count):
        p = (STEPS - 1 - start) // SWEEPS
        lo, hi = start + 2, EX - 3 - start

        def sweep(s, carry):
            def load(k):
                c = prec[p, k]
                a, b = c * adj[0, k], c * adj[1, k]
                if W <= k < W + CX:
                    gather(STEPS - 1 - s, k, a, b)
                return a, b

            def use(k, first, second, a, b):
                d = keep_c[p, k]
                adj[0, k] = d * adj[0, k] - first
                adj[1, k] = d * adj[1, k] - second

            stencil(load, p, lo, hi, use)
            return carry

        lax.fori_loop(start, start + count, sweep, 0)

    for start, count in BACKWARD:
        backward(start, count)
    for k in range(W, W + CX):
        c = prec[0, k]
        gather(0, k, c * adj[0, k], c * adj[1, k])

    grads2 = grads.reshape(3 * CX * SEG, LANES)
    for r in range(CX // 8):
        for m in range(CY // LANES):
            rows, at = pl.ds(8 * r, 8), pl.ds(LANES * m, LANES)
            stress_out[0, rows, at] = collect(grads2, 0, r, m)
            stress_out[1, rows, at] = collect(grads2, CX, r, m)
            grad_n[rows, at] = fric[rows, at] * collect(grads2, 2 * CX, r, m)

    bins = jnp.zeros((3 * n_tile, LANES), F32)
    for r in range(CX):
        high = (elem[pl.ds(r, 1), :] - first_element) // LANES
        chosen = iota((n_tile, CY), 0) == high
        value = jnp.where(chosen, grad_n[pl.ds(r, 1), :], 0.0)
        bins = bins + lax.dot_general(
            jnp.concatenate(pieces(value), axis=0), one_lo[r], (((1,), (1,)), ((), ())),
            preferred_element_type=F32,
        )
    bins = bins[:n_tile] + bins[n_tile : 2 * n_tile] + bins[2 * n_tile :]
    for k in range(n_tile):
        elem_s[k] = bins[k : k + 1, :]

    def send_bins(step, carry):
        to = lax.rem(t + step, n_tile)
        pltpu.make_async_remote_copy(
            src_ref=elem_s.at[to], dst_ref=elem_r.at[t], send_sem=el_send, recv_sem=el_recv,
            device_id=(g, to), device_id_type=MESH,
        ).start()
        return carry

    lax.fori_loop(1, n_tile, send_bins, 0)
    elem_r[t] = elem_s[t]
    pltpu.make_async_remote_copy(
        src_ref=elem_s.at[everyone], dst_ref=elem_r.at[everyone], send_sem=el_send, recv_sem=el_recv,
        device_id=(g, t), device_id_type=MESH,
    ).wait()
    result = elem_r[0]
    for k in range(1, n_tile):
        result = result + elem_r[k]
    elem_out[...] = result
    leave(moves)
    leave(amoves)


def shards(vel, stress, visc, fric, elem, observed, look, row_owner, row_cell):
    n_grp, n_tile = lax.axis_size("grp"), lax.axis_size("tile")
    rows = observed.shape[0]
    vmem = pl.BlockSpec(memory_space=pltpu.VMEM)
    outgoing = pl.pallas_call(
        functools.partial(rows_kernel, n_grp, n_tile),
        out_shape=jax.ShapeDtypeStruct((n_tile, 8, LANES), F32),
        in_specs=[vmem] * 4,
        out_specs=vmem,
        compiler_params=pltpu.CompilerParams(vmem_limit_bytes=32 << 20),
        name="rows",
    )(look, observed, row_owner.reshape(1, rows), row_cell.reshape(1, rows))
    coefficient = pltpu.VMEM((PICARD, EX, SEG, LANES), F32)
    edge, side = pltpu.VMEM((CX, LANES), F32), pltpu.VMEM((EX, LANES), F32)
    dma = pltpu.SemaphoreType.DMA
    sources = n_grp * n_tile
    stress_adjoint, elements = pl.pallas_call(
        functools.partial(main_kernel, n_grp, n_tile),
        out_shape=(
            jax.ShapeDtypeStruct((2, CX, CY), F32),
            jax.ShapeDtypeStruct((1, LANES), F32),
        ),
        in_specs=[vmem] * 6,
        out_specs=(vmem, vmem),
        scratch_shapes=[
            edge, edge,
            pltpu.VMEM((NF, W, CY), F32), pltpu.VMEM((NF, W, CY), F32),
            side, side,
            pltpu.VMEM((2, CX, CY), F32), pltpu.VMEM((2, W, CY), F32), pltpu.VMEM((2, W, CY), F32),
            edge, edge, side, side,
            pltpu.VMEM((n_tile, 8, LANES), F32),
            pltpu.VMEM((n_grp, n_tile, LANES), F32), pltpu.VMEM((n_grp, n_tile, LANES), F32),
            pltpu.VMEM((15 * CX, SLOTS * sources), BF16), pltpu.VMEM((CY, SLOTS * sources), BF16),
            pltpu.VMEM((5 * CX, CY), F32),
            pltpu.VMEM((NF, EX, SEG, LANES), F32),
            coefficient, coefficient, coefficient, coefficient, coefficient, coefficient,
            pltpu.VMEM((STEPS, 2, CX, SEG, LANES), F32),
            pltpu.VMEM((2, EX, SEG, LANES), F32),
            pltpu.VMEM((3, CX, SEG, LANES), F32),
            pltpu.VMEM((CX, CY), F32),
            pltpu.VMEM((CX, LANES, CY), BF16),
            pltpu.VMEM((n_tile, 1, LANES), F32), pltpu.VMEM((n_tile, 1, LANES), F32),
            dma((14,)), dma((14,)), dma((8,)), dma((8,)),
            dma, dma, dma((n_grp - 1,)), dma((n_grp - 1,)), dma, dma,
        ],
        compiler_params=pltpu.CompilerParams(
            collective_id=0, has_side_effects=True, vmem_limit_bytes=48 << 20
        ),
        name="adjoint",
    )(vel, stress, visc, fric, elem, outgoing)
    return stress_adjoint, elements.reshape(LANES)


def solution(mesh):
    both = ("grp", "tile")
    return jax.shard_map(
        shards,
        mesh=mesh,
        in_specs=(
            P(None, "grp", "tile"),
            P(None, "grp", "tile"),
            P(None, "grp", "tile"),
            P("grp", "tile"),
            P("grp", "tile"),
            P(both, None),
            P(None, both, None),
            P(both, None),
            P(both),
        ),
        out_specs=(P(None, "grp", "tile"), P(both)),
        check_vma=False,
    )
```

```python
import functools

import jax
import jax.numpy as jnp
from jax import lax
from jax.experimental import pallas as pl
from jax.experimental.pallas import tpu as pltpu
from jax.sharding import PartitionSpec as P

MESH = pl.DeviceIdType.MESH
CX, CY = 32, 512
SWEEPS, PICARD = 8, 2
STEPS = SWEEPS * PICARD
W = 16
EX = CX + 2 * W
SEG = 8
LANES = 128
NF = 7
SLOTS = 8
F32, BF16, I32 = jnp.float32, jnp.bfloat16, jnp.int32
FORWARD = tuple((start, 2) for start in range(0, STEPS, 2))
BACKWARD = tuple((start, min(2, STEPS - 1 - start)) for start in range(0, STEPS - 1, 2))
WHOLE = 34


def roll(x, amount):
    return pltpu.roll(x, amount % LANES, 1)


def right(x):
    return roll(x, -1)


def left(x):
    return roll(x, 1)


def pieces(x):
    high = x.astype(BF16)
    rest = x - high.astype(F32)
    middle = rest.astype(BF16)
    return high, middle, (rest - middle.astype(F32)).astype(BF16)


def iota(shape, dim):
    return lax.broadcasted_iota(I32, shape, dim)


def row_sums(n_tile, look, observed, owner, cell, out):
    rows = observed.shape[0]
    owner_row = owner[...]
    lane = iota((rows, LANES), 1)
    owner_col = jnp.transpose(jnp.broadcast_to(owner_row.astype(F32), (LANES, rows)))
    cell_col = jnp.transpose(jnp.broadcast_to(cell[...].astype(F32), (LANES, rows)))
    marks = jnp.where(owner_col == lane.astype(F32), 1.0, 0.0)
    below = jnp.where(iota((rows, rows), 0) > iota((rows, rows), 1), 1.0, 0.0).astype(BF16)
    before = jnp.dot(below, marks.astype(BF16), preferred_element_type=F32)
    rank = jnp.sum(before * marks, axis=1, keepdims=True)
    x, y, o = look[0], look[1], observed[...]
    value = cell_col
    for j, (a, b) in enumerate(((x, x), (x, y), (y, y), (x, o), (y, o))):
        value = jnp.where(lane >= SLOTS * (j + 1), jnp.sum(a * b, axis=1, keepdims=True), value)
    keep = (rank == (lane % SLOTS).astype(F32)) & (lane < SLOTS * 6)
    value = jnp.where(keep, value, 0.0)
    place = owner_row % n_tile * 8 + owner_row // n_tile
    chosen = jnp.where(iota((n_tile * 8, rows), 0) == place, 1.0, 0.0).astype(BF16)
    total = sum(jnp.dot(chosen, piece, preferred_element_type=F32) for piece in pieces(value))
    out[...] = total.reshape(n_tile, 8, LANES)


def main_kernel(
    n_grp, n_tile,
    vel_h, stress_h, visc_h, fric_h, elem_h, observed_h, look_h, owner_h, cell_h,
    stress_out, elem_out,
    vel, stress, visc, fric, elem, observed, look, owner, cell, outgoing,
    edge_l, edge_r, halo_t, halo_b, halo_l, halo_r,
    adj_n, adj_t, adj_b, aedge_l, aedge_r, ahalo_l, ahalo_r,
    first_r, second_s, second_r, gram_a, gram_b, gram,
    fields, half_q, quart_q, prec, keep_c, drive_u, drive_v,
    moments, adj, grads, grad_n, one_lo, elem_s, elem_r,
    load_sem, send_sem, recv_sem, asend_sem, arecv_sem, row_send, row_recv, grp_send, grp_recv, el_send, el_recv,
):
    g, t = lax.axis_index("grp"), lax.axis_index("tile")
    fields2 = fields.reshape(NF * EX * SEG, LANES)
    lane8 = iota((8, LANES), 1)

    pairs = (
        (vel_h, vel), (stress_h, stress), (visc_h, visc), (fric_h, fric), (owner_h, owner), (cell_h, cell),
        (look_h, look), (observed_h, observed), (elem_h, elem),
    )
    loads = [pltpu.make_async_copy(a, b, load_sem.at[i]) for i, (a, b) in enumerate(pairs)]

    barrier = pltpu.get_barrier_semaphore()
    for ref in (halo_t, halo_b, halo_l, halo_r, adj_t, adj_b, ahalo_l, ahalo_r):
        ref[...] = jnp.zeros_like(ref)

    def greet(device):
        pl.semaphore_signal(barrier, inc=1, device_id=device, device_id_type=MESH)

    up, down, west, east = g > 0, g < n_grp - 1, t > 0, t < n_tile - 1
    diagonals = ((up & west, -1, -1), (up & east, -1, 1), (down & west, 1, -1), (down & east, 1, 1))
    total = n_grp - 1 + n_tile - 1
    for there, dg, dt in diagonals:
        pl.when(there)(functools.partial(greet, (g + dg, t + dt)))
        total = total + there.astype(I32)
    greet((g, lax.rem(t + 1, n_tile)))
    greet((g, lax.rem(t + n_tile - 1, n_tile)))
    for step in range(1, n_grp):
        greet((lax.rem(g + step, n_grp), t))
    for load in loads:
        load.start()

    def greet_tile(step, carry):
        greet((g, lax.rem(t + step, n_tile)))
        return carry

    lax.fori_loop(2, n_tile - 1, greet_tile, 0)
    for load in loads[:4]:
        load.wait()

    natural = [(vel, 0), (vel, 1), (stress, 0), (stress, 1), (visc, 0), (visc, 1), (fric, None)]

    def tile_of(f, r, m):
        ref, index = natural[f]
        where = (pl.ds(8 * r, 8), pl.ds(LANES * m, LANES))
        return ref[where] if index is None else ref[(index,) + where]

    for r in range(CX // 8):
        low, high = None, None
        for f in range(NF):
            a = roll(tile_of(f, r, 0), 16 * f)
            b = roll(tile_of(f, r, CY // LANES - 1), 16 * f + 16)
            low = a if low is None else jnp.where(lane8 >= 16 * f, a, low)
            high = b if high is None else jnp.where(lane8 >= 16 * f, b, high)
        edge_l[pl.ds(8 * r, 8), :] = low
        edge_r[pl.ds(8 * r, 8), :] = high

    pl.semaphore_wait(barrier, total)

    def neighbours(blocks, e_l, e_r, h_l, h_r, send, recv):
        moves = []
        for ref, h_t, h_b in blocks:
            moves.append((down, up, ref(W), h_t, (g + 1, t)))
            moves.append((up, down, ref(0), h_b, (g - 1, t)))
        moves.append((east, west, e_r, h_l.at[pl.ds(W, CX)], (g, t + 1)))
        moves.append((west, east, e_l, h_r.at[pl.ds(W, CX)], (g, t - 1)))
        last, head, foot = pl.ds(W, W), pl.ds(0, W), pl.ds(W + CX, W)
        moves.append((down & east, up & west, e_r.at[last], h_l.at[head], (g + 1, t + 1)))
        moves.append((up & east, down & west, e_r.at[head], h_l.at[foot], (g - 1, t + 1)))
        moves.append((down & west, up & east, e_l.at[last], h_r.at[head], (g + 1, t - 1)))
        moves.append((up & west, down & east, e_l.at[head], h_r.at[foot], (g - 1, t - 1)))
        out = []
        for i, (sends, gets, source, target, device) in enumerate(moves):
            copy = pltpu.make_async_remote_copy(
                src_ref=source, dst_ref=target, send_sem=send.at[i], recv_sem=recv.at[i],
                device_id=device, device_id_type=MESH,
            )
            out.append((sends, gets, copy))
        return out

    def begin(moves):
        for sends, _, copy in moves:
            pl.when(sends)(copy.start)

    def arrive(moves):
        for _, gets, copy in moves:
            pl.when(gets)(copy.wait_recv)

    def leave(moves):
        for sends, _, copy in moves:
            pl.when(sends)(copy.wait_send)

    def rows_of(ref):
        if len(ref.shape) == 2:
            return lambda start: ref.at[pl.ds(start, W), :]
        return lambda start: ref.at[:, pl.ds(start, W), :]

    moves = neighbours(
        [
            (rows_of(vel_h), halo_t.at[pl.ds(0, 2)], halo_b.at[pl.ds(0, 2)]),
            (rows_of(stress_h), halo_t.at[pl.ds(2, 2)], halo_b.at[pl.ds(2, 2)]),
            (rows_of(visc_h), halo_t.at[pl.ds(4, 2)], halo_b.at[pl.ds(4, 2)]),
            (rows_of(fric_h), halo_t.at[6], halo_b.at[6]),
        ],
        edge_l, edge_r, halo_l, halo_r, send_sem, recv_sem,
    )
    begin(moves)

    for load in loads[4:]:
        load.wait()
    row_sums(n_tile, look, observed, owner, cell, outgoing)

    def send_rows(step, carry):
        to = lax.rem(t + step, n_tile)
        pltpu.make_async_remote_copy(
            src_ref=outgoing.at[to], dst_ref=first_r.at[t], send_sem=row_send, recv_sem=row_recv,
            device_id=(g, to), device_id_type=MESH,
        ).start()
        return carry

    lax.fori_loop(1, n_tile, send_rows, 0)

    first_element = g * (n_tile * LANES)
    for r in range(CX):
        low = (elem[pl.ds(r, 1), :] - first_element) % LANES
        one_lo[r] = jnp.where(iota((LANES, CY), 0) == low, 1.0, 0.0).astype(BF16)

    def spread(target, base, row, tiles, before, after):
        wide = [roll(x, 32) for x in tiles]
        back = [roll(x, -32) for x in tiles]
        for m in range(CY // LANES):
            even = jnp.where(lane8 < 32, before if m == 0 else wide[m - 1], wide[m])
            odd = jnp.where(lane8 < 96, back[m], after if m == CY // LANES - 1 else back[m + 1])
            target[pl.ds((base + row) * SEG + 2 * m, 8, stride=SEG), :] = even
            target[pl.ds((base + row) * SEG + 2 * m + 1, 8, stride=SEG), :] = odd

    def spread_block(f, r, tiles):
        at = pl.ds(8 * r, 8)
        spread(
            fields2, f * EX, 8 * r, tiles,
            roll(halo_l[at, :], 16 - 16 * f), roll(halo_r[at, :], 96 - 16 * f),
        )

    arrive(moves)
    for f in range(NF):
        for r in range(EX // 8):
            if r < W // 8:
                tiles = [halo_t[f, pl.ds(8 * r, 8), pl.ds(LANES * m, LANES)] for m in range(4)]
            elif r >= (W + CX) // 8:
                k = r - (W + CX) // 8
                tiles = [halo_b[f, pl.ds(8 * k, 8), pl.ds(LANES * m, LANES)] for m in range(4)]
            else:
                tiles = [tile_of(f, r - W // 8, m) for m in range(4)]
            spread_block(f, r, tiles)

    seg8 = iota((SEG, LANES), 0)
    inside = ((t > 0) | (seg8 > 0) | (lane8 >= 32)) & ((t < n_tile - 1) | (seg8 < SEG - 1) | (lane8 < 96))
    inside_top = inside & up
    inside_bottom = inside & down
    for p in range(PICARD):
        pair = fields[4 + p, 0]
        pair = pair + right(pair)
        q_old = None
        for k in range(EX - 1):
            other = fields[4 + p, k + 1]
            other = other + right(other)
            q = 0.25 * (pair + other)
            pair = other
            half_q[p, k] = 0.5 * q
            quart_q[p, k] = 0.25 * q
            if q_old is not None:
                both = q_old + q
                b = fields[6, k]
                diagonal = 1.25 * (both + left(both)) + b
                mask = inside_top if k < W else inside_bottom if k >= W + CX else inside
                c = jnp.where(mask, 0.45 / diagonal, 0.0)
                prec[p, k] = c
                keep_c[p, k] = jnp.where(mask, 1.0 - c * b, 0.0)
                drive_u[p, k] = c * fields[2, k]
                drive_v[p, k] = c * fields[3, k]
            q_old = q

    def stencil(load, p, lo, count, use):
        def node(k):
            a, b = load(k)
            la, lb = right(a), right(b)
            xa, yb, ya, xb = a + la, lb - b, la - a, b + lb
            return xa, yb, ya + xb, ya - xb, a, b

        def quad(k, old, new):
            xm, ym, sh = new[0] - old[0], new[1] + old[1], new[2] + old[3]
            both = xm + ym
            h = half_q[p, k]
            return h * (both + xm), h * (both + ym), quart_q[p, k] * sh

        def run(base, rows, carry):
            here, above = carry
            for r in range(rows):
                k = base + r
                after = node(k + 1)
                below = quad(k, here, after)
                dxx, myy = above[0] - below[0], above[1] + below[1]
                mxy, dxy = above[2] + below[2], above[2] - below[2]
                use(k, (dxx - mxy) + left(dxx + mxy), (dxy - myy) + left(dxy + myy), here[4], here[5])
                here, above = after, below
            return here, above

        before = node(lo - 1)
        here = node(lo)
        carry = (here, quad(lo - 1, before, here))
        if count <= WHOLE:
            run(lo, count, carry)
        else:
            rows = count // 2
            lax.fori_loop(0, 2, lambda i, carry: run(lo + i * rows, rows, carry), carry)

    inv = 1.0 / 0.45

    def forward(start, count):
        p = start // SWEEPS

        def sweep(s, carry):
            def use(k, first, second, u, v):
                c, d = prec[p, k], keep_c[p, k]
                new_u = (d * u + drive_u[p, k]) - c * first
                new_v = (d * v + drive_v[p, k]) - c * second
                fields[0, k] = new_u
                fields[1, k] = new_v
                moments[s, 0, k] = inv * new_u + (1.0 - inv) * u
                moments[s, 1, k] = inv * new_v + (1.0 - inv) * v

            stencil(lambda k: (fields[0, k], fields[1, k]), p, start + 1, EX - 2 - 2 * start, use)
            return carry

        lax.fori_loop(start, start + count, sweep, 0)

    for start, count in FORWARD[:4]:
        forward(start, count)

    everyone = pl.ds(0, n_tile - 1)
    pltpu.make_async_remote_copy(
        src_ref=outgoing.at[everyone], dst_ref=first_r.at[everyone], send_sem=row_send, recv_sem=row_recv,
        device_id=(g, t), device_id_type=MESH,
    ).wait()
    own = outgoing[t]
    first_r[t] = own
    flat_r = first_r.reshape(n_tile * 8, LANES)
    for k in range(n_grp):
        second_s[k] = flat_r[pl.ds(k, n_tile, stride=8), :]
    second_r[g] = second_s[g]

    def group_copy(step):
        to = lax.rem(g + step, n_grp)
        return pltpu.make_async_remote_copy(
            src_ref=second_s.at[to], dst_ref=second_r.at[g], send_sem=grp_send.at[step - 1],
            recv_sem=grp_recv.at[step - 1], device_id=(to, t), device_id_type=MESH,
        )

    for step in range(1, n_grp):
        group_copy(step).start()

    for start, count in FORWARD[4:6]:
        forward(start, count)

    for step in range(1, n_grp):
        group_copy(step).wait()
    sources = n_grp * n_tile
    arrived = jnp.transpose(second_r[...].reshape(sources, LANES))
    for s in range(SLOTS):
        cell = arrived[s : s + 1, :].astype(I32)
        at = pl.ds(s * sources, sources)
        gram_b[:, at] = jnp.where(iota((CY, sources), 0) == cell % CY, 1.0, 0.0).astype(BF16)
        chosen = iota((CX, sources), 0) == cell // CY
        for j in range(5):
            row = SLOTS * (j + 1) + s
            value = jnp.where(chosen, arrived[row : row + 1, :], 0.0)
            for q, piece in enumerate(pieces(value)):
                gram_a[pl.ds((q * 5 + j) * CX, CX), at] = piece
    product = lax.dot_general(
        gram_a[...], gram_b[...], (((1,), (1,)), ((), ())), preferred_element_type=F32
    )
    part = 5 * CX
    gram[...] = product[:part] + product[part : 2 * part] + product[2 * part :]

    for start, count in FORWARD[6:]:
        forward(start, count)

    def collect(source, base, r, m):
        a = source[pl.ds(base * SEG + 8 * SEG * r + 2 * m, 8, stride=SEG), :]
        b = source[pl.ds(base * SEG + 8 * SEG * r + 2 * m + 1, 8, stride=SEG), :]
        return jnp.where(lane8 < 64, roll(a, -32), roll(b, 32))

    scale = 1.0 / 16.0
    for r in range(CX // 8):
        for m in range(CY // LANES):
            u = collect(fields2, W, r, m)
            v = collect(fields2, EX + W, r, m)
            at = pl.ds(LANES * m, LANES)
            sxx, sxy, syy, sxo, syo = [gram[pl.ds(j * CX + 8 * r, 8), at] for j in range(5)]
            adj_n[0, pl.ds(8 * r, 8), at] = scale * (sxx * u + sxy * v - sxo)
            adj_n[1, pl.ds(8 * r, 8), at] = scale * (sxy * u + syy * v - syo)
        rows = pl.ds(8 * r, 8)
        aedge_l[rows, :] = jnp.where(
            lane8 < 16, adj_n[0, rows, pl.ds(0, LANES)], roll(adj_n[1, rows, pl.ds(0, LANES)], 16)
        )
        end = pl.ds(CY - LANES, LANES)
        aedge_r[rows, :] = jnp.where(
            lane8 < 16, roll(adj_n[0, rows, end], 16), roll(adj_n[1, rows, end], 32)
        )
    amoves = neighbours(
        [(rows_of(adj_n), adj_t, adj_b)], aedge_l, aedge_r, ahalo_l, ahalo_r, asend_sem, arecv_sem
    )
    begin(amoves)
    grads[...] = jnp.zeros_like(grads)
    arrive(amoves)
    adj2 = adj.reshape(2 * EX * SEG, LANES)
    for f in range(2):
        for r in range(EX // 8):
            if r < W // 8:
                source, k = adj_t, r
            elif r >= (W + CX) // 8:
                source, k = adj_b, r - (W + CX) // 8
            else:
                source, k = adj_n, r - W // 8
            tiles = [source[f, pl.ds(8 * k, 8), pl.ds(LANES * m, LANES)] for m in range(4)]
            at = pl.ds(8 * r, 8)
            spread(
                adj2, f * EX, 8 * r, tiles,
                roll(ahalo_l[at, :], 16 - 16 * f), roll(ahalo_r[at, :], 96 - 16 * f),
            )

    def gather(position, k, a, b):
        grads[0, k] = grads[0, k] + a
        grads[1, k] = grads[1, k] + b
        grads[2, k] = grads[2, k] - (a * moments[position, 0, k] + b * moments[position, 1, k])

    def backward(start, count):
        p = (STEPS - 1 - start) // SWEEPS

        def sweep(s, carry):
            def load(k):
                c = prec[p, k]
                a, b = c * adj[0, k], c * adj[1, k]
                gather(STEPS - 1 - s, k, a, b)
                return a, b

            def use(k, first, second, a, b):
                d = keep_c[p, k]
                adj[0, k] = d * adj[0, k] - first
                adj[1, k] = d * adj[1, k] - second

            stencil(load, p, start + 2, EX - 4 - 2 * start, use)
            return carry

        lax.fori_loop(start, start + count, sweep, 0)

    for start, count in BACKWARD:
        backward(start, count)
    for k in range(W, W + CX):
        c = prec[0, k]
        gather(0, k, c * adj[0, k], c * adj[1, k])

    grads2 = grads.reshape(3 * EX * SEG, LANES)
    for r in range(CX // 8):
        for m in range(CY // LANES):
            rows, at = pl.ds(8 * r, 8), pl.ds(LANES * m, LANES)
            stress_out[0, rows, at] = collect(grads2, W, r, m)
            stress_out[1, rows, at] = collect(grads2, EX + W, r, m)
            grad_n[rows, at] = fric[rows, at] * collect(grads2, 2 * EX + W, r, m)

    bins = jnp.zeros((3 * n_tile, LANES), F32)
    for r in range(CX):
        high = (elem[pl.ds(r, 1), :] - first_element) // LANES
        chosen = iota((n_tile, CY), 0) == high
        value = jnp.where(chosen, grad_n[pl.ds(r, 1), :], 0.0)
        bins = bins + lax.dot_general(
            jnp.concatenate(pieces(value), axis=0), one_lo[r], (((1,), (1,)), ((), ())),
            preferred_element_type=F32,
        )
    bins = bins[:n_tile] + bins[n_tile : 2 * n_tile] + bins[2 * n_tile :]
    for k in range(n_tile):
        elem_s[k] = bins[k : k + 1, :]

    def send_bins(step, carry):
        to = lax.rem(t + step, n_tile)
        pltpu.make_async_remote_copy(
            src_ref=elem_s.at[to], dst_ref=elem_r.at[t], send_sem=el_send, recv_sem=el_recv,
            device_id=(g, to), device_id_type=MESH,
        ).start()
        return carry

    lax.fori_loop(1, n_tile, send_bins, 0)
    elem_r[t] = elem_s[t]
    pltpu.make_async_remote_copy(
        src_ref=elem_s.at[everyone], dst_ref=elem_r.at[everyone], send_sem=el_send, recv_sem=el_recv,
        device_id=(g, t), device_id_type=MESH,
    ).wait()
    result = elem_r[0]
    for k in range(1, n_tile):
        result = result + elem_r[k]
    elem_out[...] = result
    leave(moves)
    leave(amoves)


def shards(vel, stress, visc, fric, elem, observed, look, row_owner, row_cell):
    n_grp, n_tile = lax.axis_size("grp"), lax.axis_size("tile")
    rows = observed.shape[0]
    vmem = pl.BlockSpec(memory_space=pltpu.VMEM)
    hbm = pl.BlockSpec(memory_space=pltpu.HBM)
    coefficient = pltpu.VMEM((PICARD, EX, SEG, LANES), F32)
    edge, side = pltpu.VMEM((CX, LANES), F32), pltpu.VMEM((EX, LANES), F32)
    dma = pltpu.SemaphoreType.DMA
    sources = n_grp * n_tile
    stress_adjoint, elements = pl.pallas_call(
        functools.partial(main_kernel, n_grp, n_tile),
        out_shape=(
            jax.ShapeDtypeStruct((2, CX, CY), F32),
            jax.ShapeDtypeStruct((1, LANES), F32),
        ),
        in_specs=[hbm] * 9,
        out_specs=(vmem, vmem),
        scratch_shapes=[
            pltpu.VMEM((2, CX, CY), F32), pltpu.VMEM((2, CX, CY), F32), pltpu.VMEM((2, CX, CY), F32),
            pltpu.VMEM((CX, CY), F32), pltpu.VMEM((CX, CY), I32),
            pltpu.VMEM(observed.shape, F32), pltpu.VMEM(look.shape, F32),
            pltpu.VMEM((1, rows), I32), pltpu.VMEM((1, rows), I32),
            pltpu.VMEM((n_tile, 8, LANES), F32),
            edge, edge,
            pltpu.VMEM((NF, W, CY), F32), pltpu.VMEM((NF, W, CY), F32),
            side, side,
            pltpu.VMEM((2, CX, CY), F32), pltpu.VMEM((2, W, CY), F32), pltpu.VMEM((2, W, CY), F32),
            edge, edge, side, side,
            pltpu.VMEM((n_tile, 8, LANES), F32),
            pltpu.VMEM((n_grp, n_tile, LANES), F32), pltpu.VMEM((n_grp, n_tile, LANES), F32),
            pltpu.VMEM((15 * CX, SLOTS * sources), BF16), pltpu.VMEM((CY, SLOTS * sources), BF16),
            pltpu.VMEM((5 * CX, CY), F32),
            pltpu.VMEM((NF, EX, SEG, LANES), F32),
            coefficient, coefficient, coefficient, coefficient, coefficient, coefficient,
            pltpu.VMEM((STEPS, 2, EX, SEG, LANES), F32),
            pltpu.VMEM((2, EX, SEG, LANES), F32),
            pltpu.VMEM((3, EX, SEG, LANES), F32),
            pltpu.VMEM((CX, CY), F32),
            pltpu.VMEM((CX, LANES, CY), BF16),
            pltpu.VMEM((n_tile, 1, LANES), F32), pltpu.VMEM((n_tile, 1, LANES), F32),
            dma((9,)), dma((14,)), dma((14,)), dma((8,)), dma((8,)),
            dma, dma, dma((n_grp - 1,)), dma((n_grp - 1,)), dma, dma,
        ],
        compiler_params=pltpu.CompilerParams(
            collective_id=0, has_side_effects=True, vmem_limit_bytes=56 << 20
        ),
        name="adjoint",
    )(
        vel, stress, visc, fric, elem, observed, look,
        row_owner.reshape(1, rows), row_cell.reshape(1, rows),
    )
    return stress_adjoint, elements.reshape(LANES)


def solution(mesh):
    both = ("grp", "tile")
    return jax.shard_map(
        shards,
        mesh=mesh,
        in_specs=(
            P(None, "grp", "tile"),
            P(None, "grp", "tile"),
            P(None, "grp", "tile"),
            P("grp", "tile"),
            P("grp", "tile"),
            P(both, None),
            P(None, both, None),
            P(both, None),
            P(both),
        ),
        out_specs=(P(None, "grp", "tile"), P(both)),
        check_vma=False,
    )
```

```python
import functools

import jax
import jax.numpy as jnp
from jax import lax
from jax.experimental import pallas as pl
from jax.experimental.pallas import tpu as pltpu
from jax.sharding import PartitionSpec as P

MESH = pl.DeviceIdType.MESH
CX, CY = 32, 512
SWEEPS, PICARD = 8, 2
STEPS = SWEEPS * PICARD
W = 16
EX = CX + 2 * W
SEG = 8
LANES = 128
NF = 7
SLOTS = 8
F32, BF16, I32 = jnp.float32, jnp.bfloat16, jnp.int32
FORWARD = tuple((start, 2) for start in range(0, STEPS, 2))
BACKWARD = tuple((start, min(2, STEPS - 1 - start)) for start in range(0, STEPS - 1, 2))
WHOLE = 34


def roll(x, amount):
    return pltpu.roll(x, amount % LANES, 1)


def right(x):
    return roll(x, -1)


def left(x):
    return roll(x, 1)


def pieces(x):
    high = x.astype(BF16)
    rest = x - high.astype(F32)
    middle = rest.astype(BF16)
    return high, middle, (rest - middle.astype(F32)).astype(BF16)


def iota(shape, dim):
    return lax.broadcasted_iota(I32, shape, dim)


def row_sums(n_tile, look, observed, owner, cell, out):
    rows = observed.shape[0]
    owner_row = owner[...]
    lane = iota((rows, LANES), 1)
    owner_col = jnp.transpose(jnp.broadcast_to(owner_row.astype(F32), (LANES, rows)))
    cell_col = jnp.transpose(jnp.broadcast_to(cell[...].astype(F32), (LANES, rows)))
    marks = jnp.where(owner_col == lane.astype(F32), 1.0, 0.0)
    below = jnp.where(iota((rows, rows), 0) > iota((rows, rows), 1), 1.0, 0.0).astype(BF16)
    before = jnp.dot(below, marks.astype(BF16), preferred_element_type=F32)
    rank = jnp.sum(before * marks, axis=1, keepdims=True)
    x, y, o = look[0], look[1], observed[...]
    value = cell_col
    for j, (a, b) in enumerate(((x, x), (x, y), (y, y), (x, o), (y, o))):
        value = jnp.where(lane >= SLOTS * (j + 1), jnp.sum(a * b, axis=1, keepdims=True), value)
    keep = (rank == (lane % SLOTS).astype(F32)) & (lane < SLOTS * 6)
    value = jnp.where(keep, value, 0.0)
    place = owner_row % n_tile * 8 + owner_row // n_tile
    chosen = jnp.where(iota((n_tile * 8, rows), 0) == place, 1.0, 0.0).astype(BF16)
    total = sum(jnp.dot(chosen, piece, preferred_element_type=F32) for piece in pieces(value))
    out[...] = total.reshape(n_tile, 8, LANES)


def main_kernel(
    n_grp, n_tile,
    vel_h, stress_h, visc_h, fric_h, elem_h, observed_h, look_h, owner_h, cell_h,
    stress_out, elem_out,
    vel, stress, visc, fric, elem, observed, look, owner, cell, outgoing,
    edge_l, edge_r, halo_t, halo_b, halo_l, halo_r,
    adj_n, adj_t, adj_b, aedge_l, aedge_r, ahalo_l, ahalo_r,
    first_r, second_s, second_r, gram_a, gram_b, gram,
    fields, half_q, quart_q, prec, keep_c, drive_u, drive_v,
    moments, adj, grads, grad_n, one_lo, elem_s, elem_r,
    load_sem, send_sem, recv_sem, asend_sem, arecv_sem, row_send, row_recv, grp_send, grp_recv, el_send, el_recv,
):
    g, t = lax.axis_index("grp"), lax.axis_index("tile")
    fields2 = fields.reshape(NF * EX * SEG, LANES)
    lane8 = iota((8, LANES), 1)

    pairs = (
        (vel_h, vel), (stress_h, stress), (visc_h, visc), (fric_h, fric), (owner_h, owner), (cell_h, cell),
        (look_h, look), (observed_h, observed), (elem_h, elem),
    )
    loads = [pltpu.make_async_copy(a, b, load_sem.at[i]) for i, (a, b) in enumerate(pairs)]

    barrier = pltpu.get_barrier_semaphore()
    for ref in (halo_t, halo_b, halo_l, halo_r, adj_t, adj_b, ahalo_l, ahalo_r):
        ref[...] = jnp.zeros_like(ref)

    def greet(device):
        pl.semaphore_signal(barrier, inc=1, device_id=device, device_id_type=MESH)

    up, down, west, east = g > 0, g < n_grp - 1, t > 0, t < n_tile - 1
    diagonals = ((up & west, -1, -1), (up & east, -1, 1), (down & west, 1, -1), (down & east, 1, 1))
    total = n_grp - 1 + n_tile - 1
    for there, dg, dt in diagonals:
        pl.when(there)(functools.partial(greet, (g + dg, t + dt)))
        total = total + there.astype(I32)
    greet((g, lax.rem(t + 1, n_tile)))
    greet((g, lax.rem(t + n_tile - 1, n_tile)))
    for step in range(1, n_grp):
        greet((lax.rem(g + step, n_grp), t))
    for load in loads:
        load.start()

    def greet_tile(step, carry):
        greet((g, lax.rem(t + step, n_tile)))
        return carry

    lax.fori_loop(2, n_tile - 1, greet_tile, 0)
    for load in loads[:4]:
        load.wait()

    natural = [(vel, 0), (vel, 1), (stress, 0), (stress, 1), (visc, 0), (visc, 1), (fric, None)]

    def tile_of(f, r, m):
        ref, index = natural[f]
        where = (pl.ds(8 * r, 8), pl.ds(LANES * m, LANES))
        return ref[where] if index is None else ref[(index,) + where]

    for r in range(CX // 8):
        low, high = None, None
        for f in range(NF):
            a = roll(tile_of(f, r, 0), 16 * f)
            b = roll(tile_of(f, r, CY // LANES - 1), 16 * f + 16)
            low = a if low is None else jnp.where(lane8 >= 16 * f, a, low)
            high = b if high is None else jnp.where(lane8 >= 16 * f, b, high)
        edge_l[pl.ds(8 * r, 8), :] = low
        edge_r[pl.ds(8 * r, 8), :] = high

    for load in loads[4:]:
        load.wait()
    row_sums(n_tile, look, observed, owner, cell, outgoing)
    pl.semaphore_wait(barrier, total)

    def neighbours(blocks, e_l, e_r, h_l, h_r, send, recv):
        moves = []
        moves.append((east, west, e_r, h_l.at[pl.ds(W, CX)], (g, t + 1)))
        moves.append((west, east, e_l, h_r.at[pl.ds(W, CX)], (g, t - 1)))
        last, head, foot = pl.ds(W, W), pl.ds(0, W), pl.ds(W + CX, W)
        moves.append((down & east, up & west, e_r.at[last], h_l.at[head], (g + 1, t + 1)))
        moves.append((up & east, down & west, e_r.at[head], h_l.at[foot], (g - 1, t + 1)))
        moves.append((down & west, up & east, e_l.at[last], h_r.at[head], (g + 1, t - 1)))
        moves.append((up & west, down & east, e_l.at[head], h_r.at[foot], (g - 1, t - 1)))
        for ref, h_t, h_b in blocks:
            moves.append((down, up, ref(W), h_t, (g + 1, t)))
            moves.append((up, down, ref(0), h_b, (g - 1, t)))
        out = []
        for i, (sends, gets, source, target, device) in enumerate(moves):
            copy = pltpu.make_async_remote_copy(
                src_ref=source, dst_ref=target, send_sem=send.at[i], recv_sem=recv.at[i],
                device_id=device, device_id_type=MESH,
            )
            out.append((sends, gets, copy))
        return out

    def begin(moves):
        for sends, _, copy in moves:
            pl.when(sends)(copy.start)

    def arrive(moves):
        for _, gets, copy in moves:
            pl.when(gets)(copy.wait_recv)

    def leave(moves):
        for sends, _, copy in moves:
            pl.when(sends)(copy.wait_send)

    def rows_of(ref):
        if len(ref.shape) == 2:
            return lambda start: ref.at[pl.ds(start, W), :]
        return lambda start: ref.at[:, pl.ds(start, W), :]

    moves = neighbours(
        [
            (rows_of(vel_h), halo_t.at[pl.ds(0, 2)], halo_b.at[pl.ds(0, 2)]),
            (rows_of(stress_h), halo_t.at[pl.ds(2, 2)], halo_b.at[pl.ds(2, 2)]),
            (rows_of(visc_h), halo_t.at[pl.ds(4, 2)], halo_b.at[pl.ds(4, 2)]),
            (rows_of(fric_h), halo_t.at[6], halo_b.at[6]),
        ],
        edge_l, edge_r, halo_l, halo_r, send_sem, recv_sem,
    )
    begin(moves)

    def send_rows(step, carry):
        to = lax.rem(t + step, n_tile)
        pltpu.make_async_remote_copy(
            src_ref=outgoing.at[to], dst_ref=first_r.at[t], send_sem=row_send, recv_sem=row_recv,
            device_id=(g, to), device_id_type=MESH,
        ).start()
        return carry

    lax.fori_loop(1, n_tile, send_rows, 0)

    first_element = g * (n_tile * LANES)
    for r in range(CX):
        low = (elem[pl.ds(r, 1), :] - first_element) % LANES
        one_lo[r] = jnp.where(iota((LANES, CY), 0) == low, 1.0, 0.0).astype(BF16)

    def spread(target, base, row, tiles, before, after):
        wide = [roll(x, 32) for x in tiles]
        back = [roll(x, -32) for x in tiles]
        for m in range(CY // LANES):
            even = jnp.where(lane8 < 32, before if m == 0 else wide[m - 1], wide[m])
            odd = jnp.where(lane8 < 96, back[m], after if m == CY // LANES - 1 else back[m + 1])
            target[pl.ds((base + row) * SEG + 2 * m, 8, stride=SEG), :] = even
            target[pl.ds((base + row) * SEG + 2 * m + 1, 8, stride=SEG), :] = odd

    def spread_block(f, r, tiles):
        at = pl.ds(8 * r, 8)
        spread(
            fields2, f * EX, 8 * r, tiles,
            roll(halo_l[at, :], 16 - 16 * f), roll(halo_r[at, :], 96 - 16 * f),
        )

    arrive(moves)
    for f in range(NF):
        for r in range(EX // 8):
            if r < W // 8:
                tiles = [halo_t[f, pl.ds(8 * r, 8), pl.ds(LANES * m, LANES)] for m in range(4)]
            elif r >= (W + CX) // 8:
                k = r - (W + CX) // 8
                tiles = [halo_b[f, pl.ds(8 * k, 8), pl.ds(LANES * m, LANES)] for m in range(4)]
            else:
                tiles = [tile_of(f, r - W // 8, m) for m in range(4)]
            spread_block(f, r, tiles)

    seg8 = iota((SEG, LANES), 0)
    inside = ((t > 0) | (seg8 > 0) | (lane8 >= 32)) & ((t < n_tile - 1) | (seg8 < SEG - 1) | (lane8 < 96))
    inside_top = inside & up
    inside_bottom = inside & down
    for p in range(PICARD):
        pair = fields[4 + p, 0]
        pair = pair + right(pair)
        q_old = None
        for k in range(EX - 1):
            other = fields[4 + p, k + 1]
            other = other + right(other)
            q = 0.25 * (pair + other)
            pair = other
            half_q[p, k] = 0.5 * q
            quart_q[p, k] = 0.25 * q
            if q_old is not None:
                both = q_old + q
                b = fields[6, k]
                diagonal = 1.25 * (both + left(both)) + b
                mask = inside_top if k < W else inside_bottom if k >= W + CX else inside
                c = jnp.where(mask, 0.45 / diagonal, 0.0)
                prec[p, k] = c
                keep_c[p, k] = jnp.where(mask, 1.0 - c * b, 0.0)
                drive_u[p, k] = c * fields[2, k]
                drive_v[p, k] = c * fields[3, k]
            q_old = q

    def stencil(load, p, lo, count, use):
        def node(k):
            a, b = load(k)
            la, lb = right(a), right(b)
            xa, yb, ya, xb = a + la, lb - b, la - a, b + lb
            return xa, yb, ya + xb, ya - xb, a, b

        def quad(k, old, new):
            xm, ym, sh = new[0] - old[0], new[1] + old[1], new[2] + old[3]
            both = xm + ym
            h = half_q[p, k]
            return h * (both + xm), h * (both + ym), quart_q[p, k] * sh

        def run(base, rows, carry):
            here, above = carry
            for r in range(rows):
                k = base + r
                after = node(k + 1)
                below = quad(k, here, after)
                dxx, myy = above[0] - below[0], above[1] + below[1]
                mxy, dxy = above[2] + below[2], above[2] - below[2]
                use(k, (dxx - mxy) + left(dxx + mxy), (dxy - myy) + left(dxy + myy), here[4], here[5])
                here, above = after, below
            return here, above

        before = node(lo - 1)
        here = node(lo)
        carry = (here, quad(lo - 1, before, here))
        if count <= WHOLE:
            run(lo, count, carry)
        else:
            rows = count // 2
            lax.fori_loop(0, 2, lambda i, carry: run(lo + i * rows, rows, carry), carry)

    inv = 1.0 / 0.45

    def forward(start, count):
        p = start // SWEEPS

        def sweep(s, carry):
            def use(k, first, second, u, v):
                c, d = prec[p, k], keep_c[p, k]
                new_u = (d * u + drive_u[p, k]) - c * first
                new_v = (d * v + drive_v[p, k]) - c * second
                fields[0, k] = new_u
                fields[1, k] = new_v
                moments[s, 0, k] = inv * new_u + (1.0 - inv) * u
                moments[s, 1, k] = inv * new_v + (1.0 - inv) * v

            stencil(lambda k: (fields[0, k], fields[1, k]), p, start + 1, EX - 2 - 2 * start, use)
            return carry

        lax.fori_loop(start, start + count, sweep, 0)

    for start, count in FORWARD[:2]:
        forward(start, count)

    everyone = pl.ds(0, n_tile - 1)
    pltpu.make_async_remote_copy(
        src_ref=outgoing.at[everyone], dst_ref=first_r.at[everyone], send_sem=row_send, recv_sem=row_recv,
        device_id=(g, t), device_id_type=MESH,
    ).wait()
    own = outgoing[t]
    first_r[t] = own
    flat_r = first_r.reshape(n_tile * 8, LANES)
    for k in range(n_grp):
        second_s[k] = flat_r[pl.ds(k, n_tile, stride=8), :]
    second_r[g] = second_s[g]

    def group_copy(step):
        to = lax.rem(g + step, n_grp)
        return pltpu.make_async_remote_copy(
            src_ref=second_s.at[to], dst_ref=second_r.at[g], send_sem=grp_send.at[step - 1],
            recv_sem=grp_recv.at[step - 1], device_id=(to, t), device_id_type=MESH,
        )

    for step in range(1, n_grp):
        group_copy(step).start()

    for start, count in FORWARD[2:6]:
        forward(start, count)

    for step in range(1, n_grp):
        group_copy(step).wait()
    sources = n_grp * n_tile
    arrived = jnp.transpose(second_r[...].reshape(sources, LANES))
    for s in range(SLOTS):
        spot = arrived[s : s + 1, :].astype(I32)
        at = pl.ds(s * sources, sources)
        gram_b[:, at] = jnp.where(iota((CY, sources), 0) == spot % CY, 1.0, 0.0).astype(BF16)
        chosen = iota((CX, sources), 0) == spot // CY
        for j in range(5):
            row = SLOTS * (j + 1) + s
            value = jnp.where(chosen, arrived[row : row + 1, :], 0.0)
            for q, piece in enumerate(pieces(value)):
                gram_a[pl.ds((q * 5 + j) * CX, CX), at] = piece
    product = lax.dot_general(
        gram_a[...], gram_b[...], (((1,), (1,)), ((), ())), preferred_element_type=F32
    )
    part = 5 * CX
    gram[...] = product[:part] + product[part : 2 * part] + product[2 * part :]

    for start, count in FORWARD[6:]:
        forward(start, count)

    def collect(source, base, r, m):
        a = source[pl.ds(base * SEG + 8 * SEG * r + 2 * m, 8, stride=SEG), :]
        b = source[pl.ds(base * SEG + 8 * SEG * r + 2 * m + 1, 8, stride=SEG), :]
        return jnp.where(lane8 < 64, roll(a, -32), roll(b, 32))

    scale = 1.0 / 16.0
    for r in range(CX // 8):
        for m in range(CY // LANES):
            u = collect(fields2, W, r, m)
            v = collect(fields2, EX + W, r, m)
            at = pl.ds(LANES * m, LANES)
            sxx, sxy, syy, sxo, syo = [gram[pl.ds(j * CX + 8 * r, 8), at] for j in range(5)]
            adj_n[0, pl.ds(8 * r, 8), at] = scale * (sxx * u + sxy * v - sxo)
            adj_n[1, pl.ds(8 * r, 8), at] = scale * (sxy * u + syy * v - syo)
        rows = pl.ds(8 * r, 8)
        aedge_l[rows, :] = jnp.where(
            lane8 < 16, adj_n[0, rows, pl.ds(0, LANES)], roll(adj_n[1, rows, pl.ds(0, LANES)], 16)
        )
        end = pl.ds(CY - LANES, LANES)
        aedge_r[rows, :] = jnp.where(
            lane8 < 16, roll(adj_n[0, rows, end], 16), roll(adj_n[1, rows, end], 32)
        )
    amoves = neighbours(
        [(rows_of(adj_n), adj_t, adj_b)], aedge_l, aedge_r, ahalo_l, ahalo_r, asend_sem, arecv_sem
    )
    begin(amoves)
    grads[...] = jnp.zeros_like(grads)
    arrive(amoves)
    adj2 = adj.reshape(2 * EX * SEG, LANES)
    for f in range(2):
        for r in range(EX // 8):
            if r < W // 8:
                source, k = adj_t, r
            elif r >= (W + CX) // 8:
                source, k = adj_b, r - (W + CX) // 8
            else:
                source, k = adj_n, r - W // 8
            tiles = [source[f, pl.ds(8 * k, 8), pl.ds(LANES * m, LANES)] for m in range(4)]
            at = pl.ds(8 * r, 8)
            spread(
                adj2, f * EX, 8 * r, tiles,
                roll(ahalo_l[at, :], 16 - 16 * f), roll(ahalo_r[at, :], 96 - 16 * f),
            )

    def gather(position, k, a, b):
        grads[0, k] = grads[0, k] + a
        grads[1, k] = grads[1, k] + b
        grads[2, k] = grads[2, k] - (a * moments[position, 0, k] + b * moments[position, 1, k])

    def backward(start, count):
        p = (STEPS - 1 - start) // SWEEPS

        def sweep(s, carry):
            def load(k):
                c = prec[p, k]
                a, b = c * adj[0, k], c * adj[1, k]
                gather(STEPS - 1 - s, k, a, b)
                return a, b

            def use(k, first, second, a, b):
                d = keep_c[p, k]
                adj[0, k] = d * adj[0, k] - first
                adj[1, k] = d * adj[1, k] - second

            stencil(load, p, start + 2, EX - 4 - 2 * start, use)
            return carry

        lax.fori_loop(start, start + count, sweep, 0)

    for start, count in BACKWARD:
        backward(start, count)
    for k in range(W, W + CX):
        c = prec[0, k]
        gather(0, k, c * adj[0, k], c * adj[1, k])

    grads2 = grads.reshape(3 * EX * SEG, LANES)
    for r in range(CX // 8):
        for m in range(CY // LANES):
            rows, at = pl.ds(8 * r, 8), pl.ds(LANES * m, LANES)
            grad_n[rows, at] = fric[rows, at] * collect(grads2, 2 * EX + W, r, m)

    bins = jnp.zeros((3 * n_tile, LANES), F32)
    for r in range(CX):
        high = (elem[pl.ds(r, 1), :] - first_element) // LANES
        chosen = iota((n_tile, CY), 0) == high
        value = jnp.where(chosen, grad_n[pl.ds(r, 1), :], 0.0)
        bins = bins + lax.dot_general(
            jnp.concatenate(pieces(value), axis=0), one_lo[r], (((1,), (1,)), ((), ())),
            preferred_element_type=F32,
        )
    bins = bins[:n_tile] + bins[n_tile : 2 * n_tile] + bins[2 * n_tile :]
    for k in range(n_tile):
        elem_s[k] = bins[k : k + 1, :]

    def send_bins(step, carry):
        to = lax.rem(t + step, n_tile)
        pltpu.make_async_remote_copy(
            src_ref=elem_s.at[to], dst_ref=elem_r.at[t], send_sem=el_send, recv_sem=el_recv,
            device_id=(g, to), device_id_type=MESH,
        ).start()
        return carry

    lax.fori_loop(1, n_tile, send_bins, 0)
    elem_r[t] = elem_s[t]
    for r in range(CX // 8):
        for m in range(CY // LANES):
            rows, at = pl.ds(8 * r, 8), pl.ds(LANES * m, LANES)
            stress_out[0, rows, at] = collect(grads2, W, r, m)
            stress_out[1, rows, at] = collect(grads2, EX + W, r, m)
    pltpu.make_async_remote_copy(
        src_ref=elem_s.at[everyone], dst_ref=elem_r.at[everyone], send_sem=el_send, recv_sem=el_recv,
        device_id=(g, t), device_id_type=MESH,
    ).wait()
    result = elem_r[0]
    for k in range(1, n_tile):
        result = result + elem_r[k]
    elem_out[...] = result.reshape(LANES)
    leave(moves)
    leave(amoves)


def shards(vel, stress, visc, fric, elem, observed, look, row_owner, row_cell):
    n_grp, n_tile = lax.axis_size("grp"), lax.axis_size("tile")
    rows = observed.shape[0]
    vmem = pl.BlockSpec(memory_space=pltpu.VMEM)
    hbm = pl.BlockSpec(memory_space=pltpu.HBM)
    coefficient = pltpu.VMEM((PICARD, EX, SEG, LANES), F32)
    edge, side = pltpu.VMEM((CX, LANES), F32), pltpu.VMEM((EX, LANES), F32)
    dma = pltpu.SemaphoreType.DMA
    sources = n_grp * n_tile
    stress_adjoint, elements = pl.pallas_call(
        functools.partial(main_kernel, n_grp, n_tile),
        out_shape=(
            jax.ShapeDtypeStruct((2, CX, CY), F32),
            jax.ShapeDtypeStruct((LANES,), F32),
        ),
        in_specs=[hbm] * 9,
        out_specs=(vmem, vmem),
        scratch_shapes=[
            pltpu.VMEM((2, CX, CY), F32), pltpu.VMEM((2, CX, CY), F32), pltpu.VMEM((2, CX, CY), F32),
            pltpu.VMEM((CX, CY), F32), pltpu.VMEM((CX, CY), I32),
            pltpu.VMEM(observed.shape, F32), pltpu.VMEM(look.shape, F32),
            pltpu.VMEM((1, rows), I32), pltpu.VMEM((1, rows), I32),
            pltpu.VMEM((n_tile, 8, LANES), F32),
            edge, edge,
            pltpu.VMEM((NF, W, CY), F32), pltpu.VMEM((NF, W, CY), F32),
            side, side,
            pltpu.VMEM((2, CX, CY), F32), pltpu.VMEM((2, W, CY), F32), pltpu.VMEM((2, W, CY), F32),
            edge, edge, side, side,
            pltpu.VMEM((n_tile, 8, LANES), F32),
            pltpu.VMEM((n_grp, n_tile, LANES), F32), pltpu.VMEM((n_grp, n_tile, LANES), F32),
            pltpu.VMEM((15 * CX, SLOTS * sources), BF16), pltpu.VMEM((CY, SLOTS * sources), BF16),
            pltpu.VMEM((5 * CX, CY), F32),
            pltpu.VMEM((NF, EX, SEG, LANES), F32),
            coefficient, coefficient, coefficient, coefficient, coefficient, coefficient,
            pltpu.VMEM((STEPS, 2, EX, SEG, LANES), F32),
            pltpu.VMEM((2, EX, SEG, LANES), F32),
            pltpu.VMEM((3, EX, SEG, LANES), F32),
            pltpu.VMEM((CX, CY), F32),
            pltpu.VMEM((CX, LANES, CY), BF16),
            pltpu.VMEM((n_tile, 1, LANES), F32), pltpu.VMEM((n_tile, 1, LANES), F32),
            dma((9,)), dma((14,)), dma((14,)), dma((8,)), dma((8,)),
            dma, dma, dma((n_grp - 1,)), dma((n_grp - 1,)), dma, dma,
        ],
        compiler_params=pltpu.CompilerParams(
            collective_id=0, has_side_effects=True, vmem_limit_bytes=56 << 20
        ),
        name="adjoint",
    )(
        vel, stress, visc, fric, elem, observed, look,
        row_owner.reshape(1, rows), row_cell.reshape(1, rows),
    )
    return stress_adjoint, elements


def solution(mesh):
    both = ("grp", "tile")
    return jax.shard_map(
        shards,
        mesh=mesh,
        in_specs=(
            P(None, "grp", "tile"),
            P(None, "grp", "tile"),
            P(None, "grp", "tile"),
            P("grp", "tile"),
            P("grp", "tile"),
            P(both, None),
            P(None, both, None),
            P(both, None),
            P(both),
        ),
        out_specs=(P(None, "grp", "tile"), P(both)),
        check_vma=False,
    )
```

```python
import functools

import jax
import jax.numpy as jnp
from jax import lax
from jax.experimental import pallas as pl
from jax.experimental.pallas import tpu as pltpu
from jax.sharding import PartitionSpec as P

MESH = pl.DeviceIdType.MESH
CX, CY = 32, 512
SWEEPS, PICARD = 8, 2
STEPS = SWEEPS * PICARD
W = 16
EX = CX + 2 * W
SEG = 8
LANES = 128
NF = 7
SLOTS = 8
F32, BF16, I32 = jnp.float32, jnp.bfloat16, jnp.int32
FORWARD = tuple((start, 1) for start in range(STEPS - 2)) + ((STEPS - 2, 2),)
BACKWARD = tuple((start, 1) for start in range(STEPS - 3)) + ((STEPS - 3, 2),)
HOPS = sorted(
    [(x, y, z) for x in range(4) for y in range(4) for z in range(2) if x + y + z],
    key=lambda d: -(min(d[0], 4 - d[0]) + min(d[1], 4 - d[1]) + 2 * d[2]),
)
WHOLE = 34


def roll(x, amount):
    return pltpu.roll(x, amount % LANES, 1)


def right(x):
    return roll(x, -1)


def left(x):
    return roll(x, 1)


def pieces(x):
    high = x.astype(BF16)
    rest = x - high.astype(F32)
    middle = rest.astype(BF16)
    return high, middle, (rest - middle.astype(F32)).astype(BF16)


def iota(shape, dim):
    return lax.broadcasted_iota(I32, shape, dim)


def row_sums(n_tile, look, observed, owner, cell, out):
    rows = observed.shape[0]
    owner_row = owner[...]
    lane = iota((rows, LANES), 1)
    owner_col = jnp.transpose(jnp.broadcast_to(owner_row.astype(F32), (LANES, rows)))
    cell_col = jnp.transpose(jnp.broadcast_to(cell[...].astype(F32), (LANES, rows)))
    marks = jnp.where(owner_col == lane.astype(F32), 1.0, 0.0)
    below = jnp.where(iota((rows, rows), 0) > iota((rows, rows), 1), 1.0, 0.0).astype(BF16)
    before = jnp.dot(below, marks.astype(BF16), preferred_element_type=F32)
    rank = jnp.sum(before * marks, axis=1, keepdims=True)
    x, y, o = look[0], look[1], observed[...]
    value = cell_col
    for j, (a, b) in enumerate(((x, x), (x, y), (y, y), (x, o), (y, o))):
        value = jnp.where(lane >= SLOTS * (j + 1), jnp.sum(a * b, axis=1, keepdims=True), value)
    keep = (rank == (lane % SLOTS).astype(F32)) & (lane < SLOTS * 6)
    value = jnp.where(keep, value, 0.0)
    place = owner_row % n_tile * 8 + owner_row // n_tile
    chosen = jnp.where(iota((n_tile * 8, rows), 0) == place, 1.0, 0.0).astype(BF16)
    total = sum(jnp.dot(chosen, piece, preferred_element_type=F32) for piece in pieces(value))
    out[...] = total.reshape(n_tile, 8, LANES)


def main_kernel(
    n_grp, n_tile,
    vel_h, stress_h, visc_h, fric_h, elem_h, observed_h, look_h, owner_h, cell_h,
    stress_out, elem_out,
    vel, stress, visc, fric, elem, observed, look, owner, cell, outgoing,
    edge_l, edge_r, halo_t, halo_b, halo_l, halo_r,
    adj_n, adj_t, adj_b, aedge_l, aedge_r, ahalo_l, ahalo_r,
    first_r, second_s, second_r, gram_a, gram_b, gram,
    fields, half_q, quart_q, prec, keep_c, drive_u, drive_v,
    moments, adj, grads, grad_n, one_lo, elem_s, elem_r,
    load_sem, send_sem, recv_sem, asend_sem, arecv_sem, row_send, row_recv, grp_send, grp_recv, el_send, el_recv,
):
    g, t = lax.axis_index("grp"), lax.axis_index("tile")
    fields2 = fields.reshape(NF * EX * SEG, LANES)
    lane8 = iota((8, LANES), 1)

    pairs = (
        (vel_h, vel), (stress_h, stress), (visc_h, visc), (fric_h, fric), (owner_h, owner), (cell_h, cell),
        (look_h, look), (observed_h, observed), (elem_h, elem),
    )
    loads = [pltpu.make_async_copy(a, b, load_sem.at[i]) for i, (a, b) in enumerate(pairs)]

    barrier = pltpu.get_barrier_semaphore()
    for ref in (halo_t, halo_b, halo_l, halo_r, adj_t, adj_b, ahalo_l, ahalo_r):
        ref[...] = jnp.zeros_like(ref)

    def partner(hop):
        x, y, z = hop
        return (t // 8 + x) % 4 * 8 + (t // 2 + y) % 4 * 2 + (t + z) % 2

    def greet(device):
        pl.semaphore_signal(barrier, inc=1, device_id=device, device_id_type=MESH)

    up, down, west, east = g > 0, g < n_grp - 1, t > 0, t < n_tile - 1
    diagonals = ((up & west, -1, -1), (up & east, -1, 1), (down & west, 1, -1), (down & east, 1, 1))
    total = n_grp - 1 + n_tile - 1
    for hop in HOPS:
        greet((g, partner(hop)))
    for there, dg, dt in diagonals:
        pl.when(there)(functools.partial(greet, (g + dg, t + dt)))
        total = total + there.astype(I32)
    for step in range(1, n_grp):
        greet((lax.rem(g + step, n_grp), t))
    for load in loads:
        load.start()

    for load in loads[:4]:
        load.wait()

    natural = [(vel, 0), (vel, 1), (stress, 0), (stress, 1), (visc, 0), (visc, 1), (fric, None)]

    def tile_of(f, r, m):
        ref, index = natural[f]
        where = (pl.ds(8 * r, 8), pl.ds(LANES * m, LANES))
        return ref[where] if index is None else ref[(index,) + where]

    for r in range(CX // 8):
        low, high = None, None
        for f in range(NF):
            a = roll(tile_of(f, r, 0), 16 * f)
            b = roll(tile_of(f, r, CY // LANES - 1), 16 * f + 16)
            low = a if low is None else jnp.where(lane8 >= 16 * f, a, low)
            high = b if high is None else jnp.where(lane8 >= 16 * f, b, high)
        edge_l[pl.ds(8 * r, 8), :] = low
        edge_r[pl.ds(8 * r, 8), :] = high

    for load in loads[4:]:
        load.wait()
    row_sums(n_tile, look, observed, owner, cell, outgoing)
    pl.semaphore_wait(barrier, total)

    def neighbours(blocks, e_l, e_r, h_l, h_r, send, recv):
        moves = []
        moves.append((east, west, e_r, h_l.at[pl.ds(W, CX)], (g, t + 1)))
        moves.append((west, east, e_l, h_r.at[pl.ds(W, CX)], (g, t - 1)))
        last, head, foot = pl.ds(W, W), pl.ds(0, W), pl.ds(W + CX, W)
        moves.append((down & east, up & west, e_r.at[last], h_l.at[head], (g + 1, t + 1)))
        moves.append((up & east, down & west, e_r.at[head], h_l.at[foot], (g - 1, t + 1)))
        moves.append((down & west, up & east, e_l.at[last], h_r.at[head], (g + 1, t - 1)))
        moves.append((up & west, down & east, e_l.at[head], h_r.at[foot], (g - 1, t - 1)))
        for ref, h_t, h_b in blocks:
            moves.append((down, up, ref(W), h_t, (g + 1, t)))
            moves.append((up, down, ref(0), h_b, (g - 1, t)))
        out = []
        for i, (sends, gets, source, target, device) in enumerate(moves):
            copy = pltpu.make_async_remote_copy(
                src_ref=source, dst_ref=target, send_sem=send.at[i], recv_sem=recv.at[i],
                device_id=device, device_id_type=MESH,
            )
            out.append((sends, gets, copy))
        return out

    def begin(moves):
        for sends, _, copy in moves:
            pl.when(sends)(copy.start)

    def arrive(moves):
        for _, gets, copy in moves:
            pl.when(gets)(copy.wait_recv)

    def leave(moves):
        for sends, _, copy in moves:
            pl.when(sends)(copy.wait_send)

    def rows_of(ref):
        if len(ref.shape) == 2:
            return lambda start: ref.at[pl.ds(start, W), :]
        return lambda start: ref.at[:, pl.ds(start, W), :]

    moves = neighbours(
        [
            (rows_of(vel), halo_t.at[pl.ds(0, 2)], halo_b.at[pl.ds(0, 2)]),
            (rows_of(stress), halo_t.at[pl.ds(2, 2)], halo_b.at[pl.ds(2, 2)]),
            (rows_of(visc), halo_t.at[pl.ds(4, 2)], halo_b.at[pl.ds(4, 2)]),
            (rows_of(fric), halo_t.at[6], halo_b.at[6]),
        ],
        edge_l, edge_r, halo_l, halo_r, send_sem, recv_sem,
    )
    begin(moves)

    for hop in HOPS:
        to = partner(hop)
        pltpu.make_async_remote_copy(
            src_ref=outgoing.at[to, pl.ds(0, n_grp)], dst_ref=first_r.at[t, pl.ds(0, n_grp)], send_sem=row_send, recv_sem=row_recv,
            device_id=(g, to), device_id_type=MESH,
        ).start()

    first_element = g * (n_tile * LANES)
    for r in range(CX):
        low = (elem[pl.ds(r, 1), :] - first_element) % LANES
        one_lo[r] = jnp.where(iota((LANES, CY), 0) == low, 1.0, 0.0).astype(BF16)

    def spread(target, base, row, tiles, before, after, inner=True, outer=True):
        wide = [roll(x, 32) for x in tiles]
        back = [roll(x, -32) for x in tiles]
        for m in range(CY // LANES):
            even = jnp.where(lane8 < 32, before if m == 0 else wide[m - 1], wide[m])
            odd = jnp.where(lane8 < 96, back[m], after if m == CY // LANES - 1 else back[m + 1])
            if outer if m == 0 else inner:
                target[pl.ds((base + row) * SEG + 2 * m, 8, stride=SEG), :] = even
            if outer if m == CY // LANES - 1 else inner:
                target[pl.ds((base + row) * SEG + 2 * m + 1, 8, stride=SEG), :] = odd

    def spread_block(f, r, tiles, inner):
        at = pl.ds(8 * r, 8)
        spread(
            fields2, f * EX, 8 * r, tiles,
            roll(halo_l[at, :], 16 - 16 * f), roll(halo_r[at, :], 96 - 16 * f), inner=inner,
        )

    for f in range(NF):
        for r in range(CX // 8):
            tiles = [tile_of(f, r, m) for m in range(4)]
            spread(fields2, f * EX, W + 8 * r, tiles, tiles[0], tiles[-1], outer=False)
    arrive(moves)
    for f in range(NF):
        for r in range(EX // 8):
            if r < W // 8:
                tiles = [halo_t[f, pl.ds(8 * r, 8), pl.ds(LANES * m, LANES)] for m in range(4)]
            elif r >= (W + CX) // 8:
                k = r - (W + CX) // 8
                tiles = [halo_b[f, pl.ds(8 * k, 8), pl.ds(LANES * m, LANES)] for m in range(4)]
            else:
                tiles = [tile_of(f, r - W // 8, m) for m in range(4)]
            spread_block(f, r, tiles, not W // 8 <= r < (W + CX) // 8)

    seg8 = iota((SEG, LANES), 0)
    inside = ((t > 0) | (seg8 > 0) | (lane8 >= 32)) & ((t < n_tile - 1) | (seg8 < SEG - 1) | (lane8 < 96))
    inside_top = inside & up
    inside_bottom = inside & down
    for p in range(PICARD):
        pair = fields[4 + p, 0]
        pair = pair + right(pair)
        q_old = None
        for k in range(EX - 1):
            other = fields[4 + p, k + 1]
            other = other + right(other)
            q = 0.25 * (pair + other)
            pair = other
            half_q[p, k] = 0.5 * q
            quart_q[p, k] = 0.25 * q
            if q_old is not None:
                both = q_old + q
                b = fields[6, k]
                diagonal = 1.25 * (both + left(both)) + b
                mask = inside_top if k < W else inside_bottom if k >= W + CX else inside
                c = jnp.where(mask, 0.45 / diagonal, 0.0)
                prec[p, k] = c
                keep_c[p, k] = jnp.where(mask, 1.0 - c * b, 0.0)
                drive_u[p, k] = c * fields[2, k]
                drive_v[p, k] = c * fields[3, k]
            q_old = q

    def stencil(load, p, lo, count, use):
        def node(k):
            a, b = load(k)
            la, lb = right(a), right(b)
            xa, yb, ya, xb = a + la, lb - b, la - a, b + lb
            return xa, yb, ya + xb, ya - xb, a, b

        def quad(k, old, new):
            xm, ym, sh = new[0] - old[0], new[1] + old[1], new[2] + old[3]
            both = xm + ym
            h = half_q[p, k]
            return h * (both + xm), h * (both + ym), quart_q[p, k] * sh

        def run(base, rows, carry):
            here, above = carry
            for r in range(rows):
                k = base + r
                after = node(k + 1)
                below = quad(k, here, after)
                dxx, myy = above[0] - below[0], above[1] + below[1]
                mxy, dxy = above[2] + below[2], above[2] - below[2]
                use(k, (dxx - mxy) + left(dxx + mxy), (dxy - myy) + left(dxy + myy), here[4], here[5])
                here, above = after, below
            return here, above

        before = node(lo - 1)
        here = node(lo)
        carry = (here, quad(lo - 1, before, here))
        if count <= WHOLE:
            run(lo, count, carry)
        else:
            rows = count // 2
            lax.fori_loop(0, 2, lambda i, carry: run(lo + i * rows, rows, carry), carry)

    inv = 1.0 / 0.45

    def forward(start, count):
        p = start // SWEEPS

        def sweep(s, carry):
            def use(k, first, second, u, v):
                c, d = prec[p, k], keep_c[p, k]
                new_u = (d * u + drive_u[p, k]) - c * first
                new_v = (d * v + drive_v[p, k]) - c * second
                fields[0, k] = new_u
                fields[1, k] = new_v
                moments[s, 0, k] = inv * new_u + (1.0 - inv) * u
                moments[s, 1, k] = inv * new_v + (1.0 - inv) * v

            stencil(lambda k: (fields[0, k], fields[1, k]), p, start + 1, EX - 2 - 2 * start, use)
            return carry

        lax.fori_loop(start, start + count, sweep, 0)

    for start, count in FORWARD[:4]:
        forward(start, count)

    everyone = pl.ds(0, n_tile - 1)
    pltpu.make_async_remote_copy(
        src_ref=outgoing.at[everyone, pl.ds(0, n_grp)], dst_ref=first_r.at[everyone, pl.ds(0, n_grp)], send_sem=row_send, recv_sem=row_recv,
        device_id=(g, t), device_id_type=MESH,
    ).wait()
    own = outgoing[t]
    first_r[t] = own
    flat_r = first_r.reshape(n_tile * 8, LANES)
    for k in range(n_grp):
        second_s[k] = flat_r[pl.ds(k, n_tile, stride=8), :]
    second_r[g] = second_s[g]

    def group_copy(step):
        to = lax.rem(g + step, n_grp)
        return pltpu.make_async_remote_copy(
            src_ref=second_s.at[to], dst_ref=second_r.at[g], send_sem=grp_send.at[step - 1],
            recv_sem=grp_recv.at[step - 1], device_id=(to, t), device_id_type=MESH,
        )

    for step in range(1, n_grp):
        group_copy(step).start()

    for start, count in FORWARD[4:12]:
        forward(start, count)

    for step in range(1, n_grp):
        group_copy(step).wait()
    sources = n_grp * n_tile
    arrived = jnp.transpose(second_r[...].reshape(sources, LANES))
    for s in range(SLOTS):
        spot = arrived[s : s + 1, :].astype(I32)
        at = pl.ds(s * sources, sources)
        gram_b[:, at] = jnp.where(iota((CY, sources), 0) == spot % CY, 1.0, 0.0).astype(BF16)
        chosen = iota((CX, sources), 0) == spot // CY
        for j in range(5):
            row = SLOTS * (j + 1) + s
            value = jnp.where(chosen, arrived[row : row + 1, :], 0.0)
            for q, piece in enumerate(pieces(value)):
                gram_a[pl.ds((q * 5 + j) * CX, CX), at] = piece
    product = lax.dot_general(
        gram_a[...], gram_b[...], (((1,), (1,)), ((), ())), preferred_element_type=F32
    )
    part = 5 * CX
    gram[...] = product[:part] + product[part : 2 * part] + product[2 * part :]

    for start, count in FORWARD[12:]:
        forward(start, count)

    def collect(source, base, r, m):
        a = source[pl.ds(base * SEG + 8 * SEG * r + 2 * m, 8, stride=SEG), :]
        b = source[pl.ds(base * SEG + 8 * SEG * r + 2 * m + 1, 8, stride=SEG), :]
        return jnp.where(lane8 < 64, roll(a, -32), roll(b, 32))

    scale = 1.0 / 16.0
    for r in range(CX // 8):
        for m in range(CY // LANES):
            u = collect(fields2, W, r, m)
            v = collect(fields2, EX + W, r, m)
            at = pl.ds(LANES * m, LANES)
            sxx, sxy, syy, sxo, syo = [gram[pl.ds(j * CX + 8 * r, 8), at] for j in range(5)]
            adj_n[0, pl.ds(8 * r, 8), at] = scale * (sxx * u + sxy * v - sxo)
            adj_n[1, pl.ds(8 * r, 8), at] = scale * (sxy * u + syy * v - syo)
        rows = pl.ds(8 * r, 8)
        aedge_l[rows, :] = jnp.where(
            lane8 < 16, adj_n[0, rows, pl.ds(0, LANES)], roll(adj_n[1, rows, pl.ds(0, LANES)], 16)
        )
        end = pl.ds(CY - LANES, LANES)
        aedge_r[rows, :] = jnp.where(
            lane8 < 16, roll(adj_n[0, rows, end], 16), roll(adj_n[1, rows, end], 32)
        )
    amoves = neighbours(
        [(rows_of(adj_n), adj_t, adj_b)], aedge_l, aedge_r, ahalo_l, ahalo_r, asend_sem, arecv_sem
    )
    begin(amoves)
    grads[...] = jnp.zeros_like(grads)
    arrive(amoves)
    adj2 = adj.reshape(2 * EX * SEG, LANES)
    for f in range(2):
        for r in range(EX // 8):
            if r < W // 8:
                source, k = adj_t, r
            elif r >= (W + CX) // 8:
                source, k = adj_b, r - (W + CX) // 8
            else:
                source, k = adj_n, r - W // 8
            tiles = [source[f, pl.ds(8 * k, 8), pl.ds(LANES * m, LANES)] for m in range(4)]
            at = pl.ds(8 * r, 8)
            spread(
                adj2, f * EX, 8 * r, tiles,
                roll(ahalo_l[at, :], 16 - 16 * f), roll(ahalo_r[at, :], 96 - 16 * f),
            )

    def gather(position, k, a, b):
        grads[0, k] = grads[0, k] + a
        grads[1, k] = grads[1, k] + b
        grads[2, k] = grads[2, k] - (a * moments[position, 0, k] + b * moments[position, 1, k])

    def backward(start, count):
        p = (STEPS - 1 - start) // SWEEPS

        def sweep(s, carry):
            def load(k):
                c = prec[p, k]
                a, b = c * adj[0, k], c * adj[1, k]
                gather(STEPS - 1 - s, k, a, b)
                return a, b

            def use(k, first, second, a, b):
                d = keep_c[p, k]
                adj[0, k] = d * adj[0, k] - first
                adj[1, k] = d * adj[1, k] - second

            stencil(load, p, start + 2, EX - 4 - 2 * start, use)
            return carry

        lax.fori_loop(start, start + count, sweep, 0)

    for start, count in BACKWARD:
        backward(start, count)
    for k in range(W, W + CX):
        c = prec[0, k]
        gather(0, k, c * adj[0, k], c * adj[1, k])

    grads2 = grads.reshape(3 * EX * SEG, LANES)
    for r in range(CX // 8):
        for m in range(CY // LANES):
            rows, at = pl.ds(8 * r, 8), pl.ds(LANES * m, LANES)
            grad_n[rows, at] = fric[rows, at] * collect(grads2, 2 * EX + W, r, m)

    bins = jnp.zeros((3 * n_tile, LANES), F32)
    for r in range(CX):
        high = (elem[pl.ds(r, 1), :] - first_element) // LANES
        chosen = iota((n_tile, CY), 0) == high
        value = jnp.where(chosen, grad_n[pl.ds(r, 1), :], 0.0)
        bins = bins + lax.dot_general(
            jnp.concatenate(pieces(value), axis=0), one_lo[r], (((1,), (1,)), ((), ())),
            preferred_element_type=F32,
        )
    bins = bins[:n_tile] + bins[n_tile : 2 * n_tile] + bins[2 * n_tile :]
    for k in range(n_tile):
        elem_s[k] = bins[k : k + 1, :]

    for hop in HOPS:
        to = partner(hop)
        pltpu.make_async_remote_copy(
            src_ref=elem_s.at[to], dst_ref=elem_r.at[t], send_sem=el_send, recv_sem=el_recv,
            device_id=(g, to), device_id_type=MESH,
        ).start()
    elem_r[t] = elem_s[t]
    for r in range(CX // 8):
        for m in range(CY // LANES):
            rows, at = pl.ds(8 * r, 8), pl.ds(LANES * m, LANES)
            stress_out[0, rows, at] = collect(grads2, W, r, m)
            stress_out[1, rows, at] = collect(grads2, EX + W, r, m)
    pltpu.make_async_remote_copy(
        src_ref=elem_s.at[everyone], dst_ref=elem_r.at[everyone], send_sem=el_send, recv_sem=el_recv,
        device_id=(g, t), device_id_type=MESH,
    ).wait()
    result = elem_r[0]
    for k in range(1, n_tile):
        result = result + elem_r[k]
    elem_out[...] = result.reshape(LANES)
    leave(moves)
    leave(amoves)


def shards(vel, stress, visc, fric, elem, observed, look, row_owner, row_cell):
    n_grp, n_tile = lax.axis_size("grp"), lax.axis_size("tile")
    rows = observed.shape[0]
    vmem = pl.BlockSpec(memory_space=pltpu.VMEM)
    hbm = pl.BlockSpec(memory_space=pltpu.HBM)
    coefficient = pltpu.VMEM((PICARD, EX, SEG, LANES), F32)
    edge, side = pltpu.VMEM((CX, LANES), F32), pltpu.VMEM((EX, LANES), F32)
    dma = pltpu.SemaphoreType.DMA
    sources = n_grp * n_tile
    stress_adjoint, elements = pl.pallas_call(
        functools.partial(main_kernel, n_grp, n_tile),
        out_shape=(
            jax.ShapeDtypeStruct((2, CX, CY), F32),
            jax.ShapeDtypeStruct((LANES,), F32),
        ),
        in_specs=[hbm] * 9,
        out_specs=(vmem, vmem),
        scratch_shapes=[
            pltpu.VMEM((2, CX, CY), F32), pltpu.VMEM((2, CX, CY), F32), pltpu.VMEM((2, CX, CY), F32),
            pltpu.VMEM((CX, CY), F32), pltpu.VMEM((CX, CY), I32),
            pltpu.VMEM(observed.shape, F32), pltpu.VMEM(look.shape, F32),
            pltpu.VMEM((1, rows), I32), pltpu.VMEM((1, rows), I32),
            pltpu.VMEM((n_tile, 8, LANES), F32),
            edge, edge,
            pltpu.VMEM((NF, W, CY), F32), pltpu.VMEM((NF, W, CY), F32),
            side, side,
            pltpu.VMEM((2, CX, CY), F32), pltpu.VMEM((2, W, CY), F32), pltpu.VMEM((2, W, CY), F32),
            edge, edge, side, side,
            pltpu.VMEM((n_tile, 8, LANES), F32),
            pltpu.VMEM((n_grp, n_tile, LANES), F32), pltpu.VMEM((n_grp, n_tile, LANES), F32),
            pltpu.VMEM((15 * CX, SLOTS * sources), BF16), pltpu.VMEM((CY, SLOTS * sources), BF16),
            pltpu.VMEM((5 * CX, CY), F32),
            pltpu.VMEM((NF, EX, SEG, LANES), F32),
            coefficient, coefficient, coefficient, coefficient, coefficient, coefficient,
            pltpu.VMEM((STEPS, 2, EX, SEG, LANES), F32),
            pltpu.VMEM((2, EX, SEG, LANES), F32),
            pltpu.VMEM((3, EX, SEG, LANES), F32),
            pltpu.VMEM((CX, CY), F32),
            pltpu.VMEM((CX, LANES, CY), BF16),
            pltpu.VMEM((n_tile, 1, LANES), F32), pltpu.VMEM((n_tile, 1, LANES), F32),
            dma((9,)), dma((14,)), dma((14,)), dma((8,)), dma((8,)),
            dma, dma, dma((n_grp - 1,)), dma((n_grp - 1,)), dma, dma,
        ],
        compiler_params=pltpu.CompilerParams(
            collective_id=0, has_side_effects=True, vmem_limit_bytes=56 << 20
        ),
        name="adjoint",
    )(
        vel, stress, visc, fric, elem, observed, look,
        row_owner.reshape(1, rows), row_cell.reshape(1, rows),
    )
    return stress_adjoint, elements


def solution(mesh):
    both = ("grp", "tile")
    return jax.shard_map(
        shards,
        mesh=mesh,
        in_specs=(
            P(None, "grp", "tile"),
            P(None, "grp", "tile"),
            P(None, "grp", "tile"),
            P("grp", "tile"),
            P("grp", "tile"),
            P(both, None),
            P(None, both, None),
            P(both, None),
            P(both),
        ),
        out_specs=(P(None, "grp", "tile"), P(both)),
        check_vma=False,
    )
```

```python
import functools

import jax
import jax.numpy as jnp
from jax import lax
from jax.experimental import pallas as pl
from jax.experimental.pallas import tpu as pltpu
from jax.sharding import PartitionSpec as P

MESH = pl.DeviceIdType.MESH
CX, CY = 32, 512
SWEEPS, PICARD = 8, 2
STEPS = SWEEPS * PICARD
W = 16
EX = CX + 2 * W
SEG = 8
LANES = 128
NF = 7
SLOTS = 8
F32, BF16, I32 = jnp.float32, jnp.bfloat16, jnp.int32
FORWARD = tuple((start, 1) for start in range(STEPS - 2)) + ((STEPS - 2, 2),)
BACKWARD = tuple((start, 1) for start in range(STEPS - 3)) + ((STEPS - 3, 2),)
HOPS = sorted(
    [(x, y, z) for x in range(4) for y in range(4) for z in range(2) if x + y + z],
    key=lambda d: -(min(d[0], 4 - d[0]) + min(d[1], 4 - d[1]) + 2 * d[2]),
)
WHOLE = 34


def roll(x, amount):
    return pltpu.roll(x, amount % LANES, 1)


def right(x):
    return roll(x, -1)


def left(x):
    return roll(x, 1)


def pieces(x):
    high = x.astype(BF16)
    rest = x - high.astype(F32)
    middle = rest.astype(BF16)
    return high, middle, (rest - middle.astype(F32)).astype(BF16)


def iota(shape, dim):
    return lax.broadcasted_iota(I32, shape, dim)


def row_sums(n_tile, look, observed, owner, cell, out):
    rows = observed.shape[0]
    owner_row = owner[...]
    lane = iota((rows, LANES), 1)
    owner_col = jnp.transpose(jnp.broadcast_to(owner_row.astype(F32), (LANES, rows)))
    cell_col = jnp.transpose(jnp.broadcast_to(cell[...].astype(F32), (LANES, rows)))
    marks = jnp.where(owner_col == lane.astype(F32), 1.0, 0.0)
    below = jnp.where(iota((rows, rows), 0) > iota((rows, rows), 1), 1.0, 0.0).astype(BF16)
    before = jnp.dot(below, marks.astype(BF16), preferred_element_type=F32)
    rank = jnp.sum(before * marks, axis=1, keepdims=True)
    x, y, o = look[0], look[1], observed[...]
    value = cell_col
    for j, (a, b) in enumerate(((x, x), (x, y), (y, y), (x, o), (y, o))):
        value = jnp.where(lane >= SLOTS * (j + 1), jnp.sum(a * b, axis=1, keepdims=True), value)
    keep = (rank == (lane % SLOTS).astype(F32)) & (lane < SLOTS * 6)
    value = jnp.where(keep, value, 0.0)
    place = owner_row % n_tile * 8 + owner_row // n_tile
    chosen = jnp.where(iota((n_tile * 8, rows), 0) == place, 1.0, 0.0).astype(BF16)
    total = sum(jnp.dot(chosen, piece, preferred_element_type=F32) for piece in pieces(value))
    out[...] = total.reshape(n_tile, 8, LANES)


def main_kernel(
    n_grp, n_tile,
    vel_h, stress_h, visc_h, fric_h, elem_h, observed_h, look_h, owner_h, cell_h,
    stress_out, elem_out,
    vel, stress, visc, fric, elem, observed, look, owner, cell, outgoing,
    edge_l, edge_r, halo_t, halo_b, halo_l, halo_r,
    adj_n, adj_t, adj_b, aedge_l, aedge_r, ahalo_l, ahalo_r,
    first_r, second_s, second_r, gram_a, gram_b, gram,
    fields, half_q, quart_q, prec, keep_c, drive_u, drive_v,
    moments, adj, grads, grad_n, one_lo, elem_s, elem_r,
    load_sem, send_sem, recv_sem, asend_sem, arecv_sem, row_send, row_recv, grp_send, grp_recv, el_send, el_recv,
):
    g, t = lax.axis_index("grp"), lax.axis_index("tile")
    fields2 = fields.reshape(NF * EX * SEG, LANES)
    lane8 = iota((8, LANES), 1)

    pairs = (
        (vel_h, vel), (stress_h, stress), (visc_h, visc), (fric_h, fric), (owner_h, owner), (cell_h, cell),
        (look_h, look), (observed_h, observed), (elem_h, elem),
    )
    loads = [pltpu.make_async_copy(a, b, load_sem.at[i]) for i, (a, b) in enumerate(pairs)]

    barrier = pltpu.get_barrier_semaphore()
    for ref in (halo_t, halo_b, halo_l, halo_r, adj_t, adj_b, ahalo_l, ahalo_r):
        ref[...] = jnp.zeros_like(ref)

    def partner(hop):
        x, y, z = hop
        return (t // 8 + x) % 4 * 8 + (t // 2 + y) % 4 * 2 + (t + z) % 2

    def greet(device):
        pl.semaphore_signal(barrier, inc=1, device_id=device, device_id_type=MESH)

    up, down, west, east = g > 0, g < n_grp - 1, t > 0, t < n_tile - 1
    diagonals = ((up & west, -1, -1), (up & east, -1, 1), (down & west, 1, -1), (down & east, 1, 1))
    total = n_grp - 1 + n_tile - 1
    for hop in HOPS:
        greet((g, partner(hop)))
    for there, dg, dt in diagonals:
        pl.when(there)(functools.partial(greet, (g + dg, t + dt)))
        total = total + there.astype(I32)
    for step in range(1, n_grp):
        greet((lax.rem(g + step, n_grp), t))
    for load in loads:
        load.start()

    for load in loads[:4]:
        load.wait()

    natural = [(vel, 0), (vel, 1), (stress, 0), (stress, 1), (visc, 0), (visc, 1), (fric, None)]

    def tile_of(f, r, m):
        ref, index = natural[f]
        where = (pl.ds(8 * r, 8), pl.ds(LANES * m, LANES))
        return ref[where] if index is None else ref[(index,) + where]

    for r in range(CX // 8):
        low, high = None, None
        for f in range(NF):
            a = roll(tile_of(f, r, 0), 16 * f)
            b = roll(tile_of(f, r, CY // LANES - 1), 16 * f + 16)
            low = a if low is None else jnp.where(lane8 >= 16 * f, a, low)
            high = b if high is None else jnp.where(lane8 >= 16 * f, b, high)
        edge_l[pl.ds(8 * r, 8), :] = low
        edge_r[pl.ds(8 * r, 8), :] = high

    for load in loads[4:]:
        load.wait()
    row_sums(n_tile, look, observed, owner, cell, outgoing)
    pl.semaphore_wait(barrier, total)

    def neighbours(blocks, e_l, e_r, h_l, h_r, send, recv):
        moves = []
        moves.append((east, west, e_r, h_l.at[pl.ds(W, CX)], (g, t + 1)))
        moves.append((west, east, e_l, h_r.at[pl.ds(W, CX)], (g, t - 1)))
        last, head, foot = pl.ds(W, W), pl.ds(0, W), pl.ds(W + CX, W)
        moves.append((down & east, up & west, e_r.at[last], h_l.at[head], (g + 1, t + 1)))
        moves.append((up & east, down & west, e_r.at[head], h_l.at[foot], (g - 1, t + 1)))
        moves.append((down & west, up & east, e_l.at[last], h_r.at[head], (g + 1, t - 1)))
        moves.append((up & west, down & east, e_l.at[head], h_r.at[foot], (g - 1, t - 1)))
        for ref, h_t, h_b in blocks:
            moves.append((down, up, ref(W), h_t, (g + 1, t)))
            moves.append((up, down, ref(0), h_b, (g - 1, t)))
        out = []
        for i, (sends, gets, source, target, device) in enumerate(moves):
            copy = pltpu.make_async_remote_copy(
                src_ref=source, dst_ref=target, send_sem=send.at[i], recv_sem=recv.at[i],
                device_id=device, device_id_type=MESH,
            )
            out.append((sends, gets, copy))
        return out

    def begin(moves):
        for sends, _, copy in moves:
            pl.when(sends)(copy.start)

    def arrive(moves):
        for _, gets, copy in moves:
            pl.when(gets)(copy.wait_recv)

    def leave(moves):
        for sends, _, copy in moves:
            pl.when(sends)(copy.wait_send)

    def rows_of(ref):
        if len(ref.shape) == 2:
            return lambda start: ref.at[pl.ds(start, W), :]
        return lambda start: ref.at[:, pl.ds(start, W), :]

    moves = neighbours(
        [
            (rows_of(vel), halo_t.at[pl.ds(0, 2)], halo_b.at[pl.ds(0, 2)]),
            (rows_of(stress), halo_t.at[pl.ds(2, 2)], halo_b.at[pl.ds(2, 2)]),
            (rows_of(visc.at[0]), halo_t.at[4], halo_b.at[4]),
            (rows_of(fric), halo_t.at[6], halo_b.at[6]),
            (rows_of(visc.at[1]), halo_t.at[5], halo_b.at[5]),
        ],
        edge_l, edge_r, halo_l, halo_r, send_sem, recv_sem,
    )
    begin(moves)
    moves, late = moves[:-2], moves[-2:]

    for hop in HOPS:
        to = partner(hop)
        pltpu.make_async_remote_copy(
            src_ref=outgoing.at[to, pl.ds(0, n_grp)], dst_ref=first_r.at[t, pl.ds(0, n_grp)], send_sem=row_send, recv_sem=row_recv,
            device_id=(g, to), device_id_type=MESH,
        ).start()

    first_element = g * (n_tile * LANES)
    for r in range(CX):
        low = (elem[pl.ds(r, 1), :] - first_element) % LANES
        one_lo[r] = jnp.where(iota((LANES, CY), 0) == low, 1.0, 0.0).astype(BF16)

    def spread(target, base, row, tiles, before, after, inner=True, outer=True):
        wide = [roll(x, 32) for x in tiles]
        back = [roll(x, -32) for x in tiles]
        for m in range(CY // LANES):
            even = jnp.where(lane8 < 32, before if m == 0 else wide[m - 1], wide[m])
            odd = jnp.where(lane8 < 96, back[m], after if m == CY // LANES - 1 else back[m + 1])
            if outer if m == 0 else inner:
                target[pl.ds((base + row) * SEG + 2 * m, 8, stride=SEG), :] = even
            if outer if m == CY // LANES - 1 else inner:
                target[pl.ds((base + row) * SEG + 2 * m + 1, 8, stride=SEG), :] = odd

    def spread_block(f, r, tiles, inner):
        at = pl.ds(8 * r, 8)
        spread(
            fields2, f * EX, 8 * r, tiles,
            roll(halo_l[at, :], 16 - 16 * f), roll(halo_r[at, :], 96 - 16 * f), inner=inner,
        )

    for f in range(NF):
        for r in range(CX // 8):
            tiles = [tile_of(f, r, m) for m in range(4)]
            spread(fields2, f * EX, W + 8 * r, tiles, tiles[0], tiles[-1], outer=False)
    def settle(f):
        for r in range(EX // 8):
            inner = not W // 8 <= r < (W + CX) // 8
            if r < W // 8:
                tiles = [halo_t[f, pl.ds(8 * r, 8), pl.ds(LANES * m, LANES)] for m in range(4)]
            elif inner:
                k = r - (W + CX) // 8
                tiles = [halo_b[f, pl.ds(8 * k, 8), pl.ds(LANES * m, LANES)] for m in range(4)]
            else:
                tiles = [tile_of(f, r - W // 8, m) for m in range(4)]
            spread_block(f, r, tiles, inner)

    arrive(moves)
    for f in (0, 1, 2, 3, 4, 6):
        settle(f)

    seg8 = iota((SEG, LANES), 0)
    inside = ((t > 0) | (seg8 > 0) | (lane8 >= 32)) & ((t < n_tile - 1) | (seg8 < SEG - 1) | (lane8 < 96))
    inside_top = inside & up
    inside_bottom = inside & down
    def coefficients(p):
        pair = fields[4 + p, 0]
        pair = pair + right(pair)
        q_old = None
        for k in range(EX - 1):
            other = fields[4 + p, k + 1]
            other = other + right(other)
            q = 0.25 * (pair + other)
            pair = other
            half_q[p, k] = 0.5 * q
            quart_q[p, k] = 0.25 * q
            if q_old is not None:
                both = q_old + q
                b = fields[6, k]
                diagonal = 1.25 * (both + left(both)) + b
                mask = inside_top if k < W else inside_bottom if k >= W + CX else inside
                c = jnp.where(mask, 0.45 / diagonal, 0.0)
                prec[p, k] = c
                keep_c[p, k] = jnp.where(mask, 1.0 - c * b, 0.0)
                drive_u[p, k] = c * fields[2, k]
                drive_v[p, k] = c * fields[3, k]
            q_old = q

    coefficients(0)

    def stencil(load, p, lo, count, use):
        def node(k):
            a, b = load(k)
            la, lb = right(a), right(b)
            xa, yb, ya, xb = a + la, lb - b, la - a, b + lb
            return xa, yb, ya + xb, ya - xb, a, b

        def quad(k, old, new):
            xm, ym, sh = new[0] - old[0], new[1] + old[1], new[2] + old[3]
            both = xm + ym
            h = half_q[p, k]
            return h * (both + xm), h * (both + ym), quart_q[p, k] * sh

        def run(base, rows, carry):
            here, above = carry
            for r in range(rows):
                k = base + r
                after = node(k + 1)
                below = quad(k, here, after)
                dxx, myy = above[0] - below[0], above[1] + below[1]
                mxy, dxy = above[2] + below[2], above[2] - below[2]
                use(k, (dxx - mxy) + left(dxx + mxy), (dxy - myy) + left(dxy + myy), here[4], here[5])
                here, above = after, below
            return here, above

        before = node(lo - 1)
        here = node(lo)
        carry = (here, quad(lo - 1, before, here))
        if count <= WHOLE:
            run(lo, count, carry)
        else:
            rows = count // 2
            lax.fori_loop(0, 2, lambda i, carry: run(lo + i * rows, rows, carry), carry)

    inv = 1.0 / 0.45

    def forward(start, count):
        p = start // SWEEPS

        def sweep(s, carry):
            def use(k, first, second, u, v):
                c, d = prec[p, k], keep_c[p, k]
                new_u = (d * u + drive_u[p, k]) - c * first
                new_v = (d * v + drive_v[p, k]) - c * second
                fields[0, k] = new_u
                fields[1, k] = new_v
                moments[s, 0, k] = inv * new_u + (1.0 - inv) * u
                moments[s, 1, k] = inv * new_v + (1.0 - inv) * v

            stencil(lambda k: (fields[0, k], fields[1, k]), p, start + 1, EX - 2 - 2 * start, use)
            return carry

        lax.fori_loop(start, start + count, sweep, 0)

    for start, count in FORWARD[:4]:
        forward(start, count)

    everyone = pl.ds(0, n_tile - 1)
    pltpu.make_async_remote_copy(
        src_ref=outgoing.at[everyone, pl.ds(0, n_grp)], dst_ref=first_r.at[everyone, pl.ds(0, n_grp)], send_sem=row_send, recv_sem=row_recv,
        device_id=(g, t), device_id_type=MESH,
    ).wait()
    own = outgoing[t]
    first_r[t] = own
    flat_r = first_r.reshape(n_tile * 8, LANES)
    for k in range(n_grp):
        second_s[k] = flat_r[pl.ds(k, n_tile, stride=8), :]
    second_r[g] = second_s[g]

    def group_copy(step):
        to = lax.rem(g + step, n_grp)
        return pltpu.make_async_remote_copy(
            src_ref=second_s.at[to], dst_ref=second_r.at[g], send_sem=grp_send.at[step - 1],
            recv_sem=grp_recv.at[step - 1], device_id=(to, t), device_id_type=MESH,
        )

    for step in range(1, n_grp):
        group_copy(step).start()

    for start, count in FORWARD[4:SWEEPS]:
        forward(start, count)
    arrive(late)
    settle(5)
    coefficients(1)
    for start, count in FORWARD[SWEEPS:12]:
        forward(start, count)

    for step in range(1, n_grp):
        group_copy(step).wait()
    sources = n_grp * n_tile
    arrived = jnp.transpose(second_r[...].reshape(sources, LANES))
    for s in range(SLOTS):
        spot = arrived[s : s + 1, :].astype(I32)
        at = pl.ds(s * sources, sources)
        gram_b[:, at] = jnp.where(iota((CY, sources), 0) == spot % CY, 1.0, 0.0).astype(BF16)
        chosen = iota((CX, sources), 0) == spot // CY
        for j in range(5):
            row = SLOTS * (j + 1) + s
            value = jnp.where(chosen, arrived[row : row + 1, :], 0.0)
            for q, piece in enumerate(pieces(value)):
                gram_a[pl.ds((q * 5 + j) * CX, CX), at] = piece
    product = lax.dot_general(
        gram_a[...], gram_b[...], (((1,), (1,)), ((), ())), preferred_element_type=F32
    )
    part = 5 * CX
    gram[...] = product[:part] + product[part : 2 * part] + product[2 * part :]

    for start, count in FORWARD[12:]:
        forward(start, count)

    def collect(source, base, r, m):
        a = source[pl.ds(base * SEG + 8 * SEG * r + 2 * m, 8, stride=SEG), :]
        b = source[pl.ds(base * SEG + 8 * SEG * r + 2 * m + 1, 8, stride=SEG), :]
        return jnp.where(lane8 < 64, roll(a, -32), roll(b, 32))

    scale = 1.0 / 16.0
    for r in range(CX // 8):
        for m in range(CY // LANES):
            u = collect(fields2, W, r, m)
            v = collect(fields2, EX + W, r, m)
            at = pl.ds(LANES * m, LANES)
            sxx, sxy, syy, sxo, syo = [gram[pl.ds(j * CX + 8 * r, 8), at] for j in range(5)]
            adj_n[0, pl.ds(8 * r, 8), at] = scale * (sxx * u + sxy * v - sxo)
            adj_n[1, pl.ds(8 * r, 8), at] = scale * (sxy * u + syy * v - syo)
        rows = pl.ds(8 * r, 8)
        aedge_l[rows, :] = jnp.where(
            lane8 < 16, adj_n[0, rows, pl.ds(0, LANES)], roll(adj_n[1, rows, pl.ds(0, LANES)], 16)
        )
        end = pl.ds(CY - LANES, LANES)
        aedge_r[rows, :] = jnp.where(
            lane8 < 16, roll(adj_n[0, rows, end], 16), roll(adj_n[1, rows, end], 32)
        )
    amoves = neighbours(
        [(rows_of(adj_n), adj_t, adj_b)], aedge_l, aedge_r, ahalo_l, ahalo_r, asend_sem, arecv_sem
    )
    begin(amoves)
    grads[...] = jnp.zeros_like(grads)
    arrive(amoves)
    adj2 = adj.reshape(2 * EX * SEG, LANES)
    for f in range(2):
        for r in range(EX // 8):
            if r < W // 8:
                source, k = adj_t, r
            elif r >= (W + CX) // 8:
                source, k = adj_b, r - (W + CX) // 8
            else:
                source, k = adj_n, r - W // 8
            tiles = [source[f, pl.ds(8 * k, 8), pl.ds(LANES * m, LANES)] for m in range(4)]
            at = pl.ds(8 * r, 8)
            spread(
                adj2, f * EX, 8 * r, tiles,
                roll(ahalo_l[at, :], 16 - 16 * f), roll(ahalo_r[at, :], 96 - 16 * f),
            )

    def gather(position, k, a, b):
        grads[0, k] = grads[0, k] + a
        grads[1, k] = grads[1, k] + b
        grads[2, k] = grads[2, k] - (a * moments[position, 0, k] + b * moments[position, 1, k])

    def backward(start, count):
        p = (STEPS - 1 - start) // SWEEPS

        def sweep(s, carry):
            def load(k):
                c = prec[p, k]
                a, b = c * adj[0, k], c * adj[1, k]
                gather(STEPS - 1 - s, k, a, b)
                return a, b

            def use(k, first, second, a, b):
                d = keep_c[p, k]
                adj[0, k] = d * adj[0, k] - first
                adj[1, k] = d * adj[1, k] - second

            stencil(load, p, start + 2, EX - 4 - 2 * start, use)
            return carry

        lax.fori_loop(start, start + count, sweep, 0)

    for start, count in BACKWARD:
        backward(start, count)
    for k in range(W, W + CX):
        c = prec[0, k]
        gather(0, k, c * adj[0, k], c * adj[1, k])

    grads2 = grads.reshape(3 * EX * SEG, LANES)
    for r in range(CX // 8):
        for m in range(CY // LANES):
            rows, at = pl.ds(8 * r, 8), pl.ds(LANES * m, LANES)
            grad_n[rows, at] = fric[rows, at] * collect(grads2, 2 * EX + W, r, m)

    bins = jnp.zeros((3 * n_tile, LANES), F32)
    for r in range(CX):
        high = (elem[pl.ds(r, 1), :] - first_element) // LANES
        chosen = iota((n_tile, CY), 0) == high
        value = jnp.where(chosen, grad_n[pl.ds(r, 1), :], 0.0)
        bins = bins + lax.dot_general(
            jnp.concatenate(pieces(value), axis=0), one_lo[r], (((1,), (1,)), ((), ())),
            preferred_element_type=F32,
        )
    bins = bins[:n_tile] + bins[n_tile : 2 * n_tile] + bins[2 * n_tile :]
    for k in range(n_tile):
        elem_s[k] = bins[k : k + 1, :]

    for hop in HOPS:
        to = partner(hop)
        pltpu.make_async_remote_copy(
            src_ref=elem_s.at[to], dst_ref=elem_r.at[t], send_sem=el_send, recv_sem=el_recv,
            device_id=(g, to), device_id_type=MESH,
        ).start()
    elem_r[t] = elem_s[t]
    for r in range(CX // 8):
        for m in range(CY // LANES):
            rows, at = pl.ds(8 * r, 8), pl.ds(LANES * m, LANES)
            stress_out[0, rows, at] = collect(grads2, W, r, m)
            stress_out[1, rows, at] = collect(grads2, EX + W, r, m)
    pltpu.make_async_remote_copy(
        src_ref=elem_s.at[everyone], dst_ref=elem_r.at[everyone], send_sem=el_send, recv_sem=el_recv,
        device_id=(g, t), device_id_type=MESH,
    ).wait()
    result = elem_r[0]
    for k in range(1, n_tile):
        result = result + elem_r[k]
    elem_out[...] = result.reshape(LANES)
    leave(moves)
    leave(late)
    leave(amoves)


def shards(vel, stress, visc, fric, elem, observed, look, row_owner, row_cell):
    n_grp, n_tile = lax.axis_size("grp"), lax.axis_size("tile")
    rows = observed.shape[0]
    vmem = pl.BlockSpec(memory_space=pltpu.VMEM)
    hbm = pl.BlockSpec(memory_space=pltpu.HBM)
    coefficient = pltpu.VMEM((PICARD, EX, SEG, LANES), F32)
    edge, side = pltpu.VMEM((CX, LANES), F32), pltpu.VMEM((EX, LANES), F32)
    dma = pltpu.SemaphoreType.DMA
    sources = n_grp * n_tile
    stress_adjoint, elements = pl.pallas_call(
        functools.partial(main_kernel, n_grp, n_tile),
        out_shape=(
            jax.ShapeDtypeStruct((2, CX, CY), F32),
            jax.ShapeDtypeStruct((LANES,), F32),
        ),
        in_specs=[hbm] * 9,
        out_specs=(vmem, vmem),
        scratch_shapes=[
            pltpu.VMEM((2, CX, CY), F32), pltpu.VMEM((2, CX, CY), F32), pltpu.VMEM((2, CX, CY), F32),
            pltpu.VMEM((CX, CY), F32), pltpu.VMEM((CX, CY), I32),
            pltpu.VMEM(observed.shape, F32), pltpu.VMEM(look.shape, F32),
            pltpu.VMEM((1, rows), I32), pltpu.VMEM((1, rows), I32),
            pltpu.VMEM((n_tile, 8, LANES), F32),
            edge, edge,
            pltpu.VMEM((NF, W, CY), F32), pltpu.VMEM((NF, W, CY), F32),
            side, side,
            pltpu.VMEM((2, CX, CY), F32), pltpu.VMEM((2, W, CY), F32), pltpu.VMEM((2, W, CY), F32),
            edge, edge, side, side,
            pltpu.VMEM((n_tile, 8, LANES), F32),
            pltpu.VMEM((n_grp, n_tile, LANES), F32), pltpu.VMEM((n_grp, n_tile, LANES), F32),
            pltpu.VMEM((15 * CX, SLOTS * sources), BF16), pltpu.VMEM((CY, SLOTS * sources), BF16),
            pltpu.VMEM((5 * CX, CY), F32),
            pltpu.VMEM((NF, EX, SEG, LANES), F32),
            coefficient, coefficient, coefficient, coefficient, coefficient, coefficient,
            pltpu.VMEM((STEPS, 2, EX, SEG, LANES), F32),
            pltpu.VMEM((2, EX, SEG, LANES), F32),
            pltpu.VMEM((3, EX, SEG, LANES), F32),
            pltpu.VMEM((CX, CY), F32),
            pltpu.VMEM((CX, LANES, CY), BF16),
            pltpu.VMEM((n_tile, 1, LANES), F32), pltpu.VMEM((n_tile, 1, LANES), F32),
            dma((9,)), dma((16,)), dma((16,)), dma((8,)), dma((8,)),
            dma, dma, dma((n_grp - 1,)), dma((n_grp - 1,)), dma, dma,
        ],
        compiler_params=pltpu.CompilerParams(
            collective_id=0, has_side_effects=True, vmem_limit_bytes=56 << 20
        ),
        name="adjoint",
    )(
        vel, stress, visc, fric, elem, observed, look,
        row_owner.reshape(1, rows), row_cell.reshape(1, rows),
    )
    return stress_adjoint, elements


def solution(mesh):
    both = ("grp", "tile")
    return jax.shard_map(
        shards,
        mesh=mesh,
        in_specs=(
            P(None, "grp", "tile"),
            P(None, "grp", "tile"),
            P(None, "grp", "tile"),
            P("grp", "tile"),
            P("grp", "tile"),
            P(both, None),
            P(None, both, None),
            P(both, None),
            P(both),
        ),
        out_specs=(P(None, "grp", "tile"), P(both)),
        check_vma=False,
    )
```

```python
import functools

import jax
import jax.numpy as jnp
from jax import lax
from jax.experimental import pallas as pl
from jax.experimental.pallas import tpu as pltpu
from jax.sharding import PartitionSpec as P

MESH = pl.DeviceIdType.MESH
CX, CY = 32, 512
SWEEPS, PICARD = 8, 2
STEPS = SWEEPS * PICARD
W = 16
EX = CX + 2 * W
SEG = 8
LANES = 128
NF = 7
SLOTS = 8
F32, BF16, I32 = jnp.float32, jnp.bfloat16, jnp.int32
FORWARD = tuple((start, 1) for start in range(STEPS - 2)) + ((STEPS - 2, 2),)
BACKWARD = tuple((start, 1) for start in range(STEPS - 3)) + ((STEPS - 3, 2),)
HOPS = sorted(
    [(x, y, z) for x in range(4) for y in range(4) for z in range(2) if x + y + z],
    key=lambda d: -(min(d[0], 4 - d[0]) + min(d[1], 4 - d[1]) + 2 * d[2]),
)
WHOLE = 34


def roll(x, amount):
    return pltpu.roll(x, amount % LANES, 1)


def right(x):
    return roll(x, -1)


def left(x):
    return roll(x, 1)


def pieces(x):
    high = x.astype(BF16)
    rest = x - high.astype(F32)
    middle = rest.astype(BF16)
    return high, middle, (rest - middle.astype(F32)).astype(BF16)


def iota(shape, dim):
    return lax.broadcasted_iota(I32, shape, dim)


def row_sums(n_tile, look, observed, owner, cell, out):
    rows = observed.shape[0]
    owner_row = owner[...]
    lane = iota((rows, LANES), 1)
    owner_col = jnp.transpose(jnp.broadcast_to(owner_row.astype(F32), (LANES, rows)))
    cell_col = jnp.transpose(jnp.broadcast_to(cell[...].astype(F32), (LANES, rows)))
    marks = jnp.where(owner_col == lane.astype(F32), 1.0, 0.0)
    below = jnp.where(iota((rows, rows), 0) > iota((rows, rows), 1), 1.0, 0.0).astype(BF16)
    before = jnp.dot(below, marks.astype(BF16), preferred_element_type=F32)
    rank = jnp.sum(before * marks, axis=1, keepdims=True)
    x, y, o = look[0], look[1], observed[...]
    value = cell_col
    for j, (a, b) in enumerate(((x, x), (x, y), (y, y), (x, o), (y, o))):
        value = jnp.where(lane >= SLOTS * (j + 1), jnp.sum(a * b, axis=1, keepdims=True), value)
    keep = (rank == (lane % SLOTS).astype(F32)) & (lane < SLOTS * 6)
    value = jnp.where(keep, value, 0.0)
    place = owner_row % n_tile * 8 + owner_row // n_tile
    chosen = jnp.where(iota((n_tile * 8, rows), 0) == place, 1.0, 0.0).astype(BF16)
    total = sum(jnp.dot(chosen, piece, preferred_element_type=F32) for piece in pieces(value))
    out[...] = total.reshape(n_tile, 8, LANES)


def main_kernel(
    n_grp, n_tile,
    vel_h, stress_h, visc_h, fric_h, elem_h, observed_h, look_h, owner_h, cell_h,
    stress_out, elem_out,
    vel, stress, visc, fric, elem, observed, look, owner, cell, outgoing,
    edge_l, edge_r, halo_t, halo_b, halo_l, halo_r,
    adj_n, adj_t, adj_b, aedge_l, aedge_r, ahalo_l, ahalo_r,
    first_r, second_s, second_r, gram_a, gram_b, gram,
    fields, half_q, quart_q, prec, keep_c, drive_u, drive_v,
    moments, adj, grads, grad_n, one_lo, elem_s, elem_r,
    load_sem, send_sem, recv_sem, asend_sem, arecv_sem, row_send, row_recv, grp_send, grp_recv, el_send, el_recv,
):
    g, t = lax.axis_index("grp"), lax.axis_index("tile")
    fields2 = fields.reshape(NF * EX * SEG, LANES)
    lane8 = iota((8, LANES), 1)

    pairs = (
        (vel_h, vel), (stress_h, stress), (visc_h, visc), (fric_h, fric), (owner_h, owner), (cell_h, cell),
        (look_h, look), (observed_h, observed), (elem_h, elem),
    )
    loads = [pltpu.make_async_copy(a, b, load_sem.at[i]) for i, (a, b) in enumerate(pairs)]

    barrier = pltpu.get_barrier_semaphore()
    for ref in (halo_t, halo_b, halo_l, halo_r, adj_t, adj_b, ahalo_l, ahalo_r):
        ref[...] = jnp.zeros_like(ref)

    def partner(hop):
        x, y, z = hop
        return (t // 8 + x) % 4 * 8 + (t // 2 + y) % 4 * 2 + (t + z) % 2

    def greet(device):
        pl.semaphore_signal(barrier, inc=1, device_id=device, device_id_type=MESH)

    up, down, west, east = g > 0, g < n_grp - 1, t > 0, t < n_tile - 1
    diagonals = ((up & west, -1, -1), (up & east, -1, 1), (down & west, 1, -1), (down & east, 1, 1))
    total = n_grp - 1 + n_tile - 1
    for hop in HOPS:
        greet((g, partner(hop)))
    for there, dg, dt in diagonals:
        pl.when(there)(functools.partial(greet, (g + dg, t + dt)))
        total = total + there.astype(I32)
    for step in range(1, n_grp):
        greet((lax.rem(g + step, n_grp), t))
    for load in loads:
        load.start()

    for load in loads[:4]:
        load.wait()

    natural = [(vel, 0), (vel, 1), (stress, 0), (stress, 1), (visc, 0), (visc, 1), (fric, None)]

    def tile_of(f, r, m):
        ref, index = natural[f]
        where = (pl.ds(8 * r, 8), pl.ds(LANES * m, LANES))
        return ref[where] if index is None else ref[(index,) + where]

    for r in range(CX // 8):
        low, high = None, None
        for f in range(NF):
            a = roll(tile_of(f, r, 0), 16 * f)
            b = roll(tile_of(f, r, CY // LANES - 1), 16 * f + 16)
            low = a if low is None else jnp.where(lane8 >= 16 * f, a, low)
            high = b if high is None else jnp.where(lane8 >= 16 * f, b, high)
        edge_l[pl.ds(8 * r, 8), :] = low
        edge_r[pl.ds(8 * r, 8), :] = high

    for load in loads[4:]:
        load.wait()
    row_sums(n_tile, look, observed, owner, cell, outgoing)
    pl.semaphore_wait(barrier, total)

    def neighbours(blocks, e_l, e_r, h_l, h_r, send, recv):
        moves = []
        moves.append((east, west, e_r, h_l.at[pl.ds(W, CX)], (g, t + 1)))
        moves.append((west, east, e_l, h_r.at[pl.ds(W, CX)], (g, t - 1)))
        last, head, foot = pl.ds(W, W), pl.ds(0, W), pl.ds(W + CX, W)
        moves.append((down & east, up & west, e_r.at[last], h_l.at[head], (g + 1, t + 1)))
        moves.append((up & east, down & west, e_r.at[head], h_l.at[foot], (g - 1, t + 1)))
        moves.append((down & west, up & east, e_l.at[last], h_r.at[head], (g + 1, t - 1)))
        moves.append((up & west, down & east, e_l.at[head], h_r.at[foot], (g - 1, t - 1)))
        for ref, h_t, h_b in blocks:
            moves.append((down, up, ref(W), h_t, (g + 1, t)))
            moves.append((up, down, ref(0), h_b, (g - 1, t)))
        out = []
        for i, (sends, gets, source, target, device) in enumerate(moves):
            copy = pltpu.make_async_remote_copy(
                src_ref=source, dst_ref=target, send_sem=send.at[i], recv_sem=recv.at[i],
                device_id=device, device_id_type=MESH,
            )
            out.append((sends, gets, copy))
        return out

    def begin(moves):
        for sends, _, copy in moves:
            pl.when(sends)(copy.start)

    def arrive(moves):
        for _, gets, copy in moves:
            pl.when(gets)(copy.wait_recv)

    def leave(moves):
        for sends, _, copy in moves:
            pl.when(sends)(copy.wait_send)

    def rows_of(ref):
        if len(ref.shape) == 2:
            return lambda start: ref.at[pl.ds(start, W), :]
        return lambda start: ref.at[:, pl.ds(start, W), :]

    moves = neighbours(
        [
            (rows_of(vel), halo_t.at[pl.ds(0, 2)], halo_b.at[pl.ds(0, 2)]),
            (rows_of(stress), halo_t.at[pl.ds(2, 2)], halo_b.at[pl.ds(2, 2)]),
            (rows_of(visc.at[0]), halo_t.at[4], halo_b.at[4]),
            (rows_of(fric), halo_t.at[6], halo_b.at[6]),
            (rows_of(visc.at[1]), halo_t.at[5], halo_b.at[5]),
        ],
        edge_l, edge_r, halo_l, halo_r, send_sem, recv_sem,
    )
    begin(moves)
    moves, late = moves[:-2], moves[-2:]

    for hop in HOPS:
        to = partner(hop)
        pltpu.make_async_remote_copy(
            src_ref=outgoing.at[to, pl.ds(0, n_grp)], dst_ref=first_r.at[t, pl.ds(0, n_grp)], send_sem=row_send, recv_sem=row_recv,
            device_id=(g, to), device_id_type=MESH,
        ).start()

    first_element = g * (n_tile * LANES)
    for r in range(CX):
        low = (elem[pl.ds(r, 1), :] - first_element) % LANES
        one_lo[r] = jnp.where(iota((LANES, CY), 0) == low, 1.0, 0.0).astype(BF16)

    def spread(target, base, row, tiles, before, after, inner=True, outer=True):
        wide = [roll(x, 32) for x in tiles]
        back = [roll(x, -32) for x in tiles]
        for m in range(CY // LANES):
            even = jnp.where(lane8 < 32, before if m == 0 else wide[m - 1], wide[m])
            odd = jnp.where(lane8 < 96, back[m], after if m == CY // LANES - 1 else back[m + 1])
            if outer if m == 0 else inner:
                target[pl.ds((base + row) * SEG + 2 * m, 8, stride=SEG), :] = even
            if outer if m == CY // LANES - 1 else inner:
                target[pl.ds((base + row) * SEG + 2 * m + 1, 8, stride=SEG), :] = odd

    def spread_block(f, r, tiles, inner):
        at = pl.ds(8 * r, 8)
        spread(
            fields2, f * EX, 8 * r, tiles,
            roll(halo_l[at, :], 16 - 16 * f), roll(halo_r[at, :], 96 - 16 * f), inner=inner,
        )

    for f in range(NF):
        for r in range(CX // 8):
            tiles = [tile_of(f, r, m) for m in range(4)]
            spread(fields2, f * EX, W + 8 * r, tiles, tiles[0], tiles[-1], outer=False)
    def settle(f):
        for r in range(EX // 8):
            inner = not W // 8 <= r < (W + CX) // 8
            if r < W // 8:
                tiles = [halo_t[f, pl.ds(8 * r, 8), pl.ds(LANES * m, LANES)] for m in range(4)]
            elif inner:
                k = r - (W + CX) // 8
                tiles = [halo_b[f, pl.ds(8 * k, 8), pl.ds(LANES * m, LANES)] for m in range(4)]
            else:
                tiles = [tile_of(f, r - W // 8, m) for m in range(4)]
            spread_block(f, r, tiles, inner)

    arrive(moves)
    for f in (0, 1, 2, 3, 4, 6):
        settle(f)

    seg8 = iota((SEG, LANES), 0)
    inside = ((t > 0) | (seg8 > 0) | (lane8 >= 32)) & ((t < n_tile - 1) | (seg8 < SEG - 1) | (lane8 < 96))
    inside_top = inside & up
    inside_bottom = inside & down
    def coefficients(p):
        pair = fields[4 + p, 0]
        pair = pair + right(pair)
        q_old = None
        for k in range(EX - 1):
            other = fields[4 + p, k + 1]
            other = other + right(other)
            q = 0.25 * (pair + other)
            pair = other
            half_q[p, k] = 0.5 * q
            quart_q[p, k] = 0.25 * q
            if q_old is not None:
                both = q_old + q
                b = fields[6, k]
                diagonal = 1.25 * (both + left(both)) + b
                mask = inside_top if k < W else inside_bottom if k >= W + CX else inside
                c = jnp.where(mask, 0.45 / diagonal, 0.0)
                prec[p, k] = c
                keep_c[p, k] = jnp.where(mask, 1.0 - c * b, 0.0)
                drive_u[p, k] = c * fields[2, k]
                drive_v[p, k] = c * fields[3, k]
            q_old = q

    coefficients(0)

    def stencil(load, p, lo, count, use):
        def node(k):
            a, b = load(k)
            la, lb = right(a), right(b)
            xa, yb, ya, xb = a + la, lb - b, la - a, b + lb
            return xa, yb, ya + xb, ya - xb, a, b

        def quad(k, old, new):
            xm, ym, sh = new[0] - old[0], new[1] + old[1], new[2] + old[3]
            both = xm + ym
            h = half_q[p, k]
            return h * (both + xm), h * (both + ym), quart_q[p, k] * sh

        def run(base, rows, carry):
            here, above = carry
            for r in range(rows):
                k = base + r
                after = node(k + 1)
                below = quad(k, here, after)
                dxx, myy = above[0] - below[0], above[1] + below[1]
                mxy, dxy = above[2] + below[2], above[2] - below[2]
                use(k, (dxx - mxy) + left(dxx + mxy), (dxy - myy) + left(dxy + myy), here[4], here[5])
                here, above = after, below
            return here, above

        before = node(lo - 1)
        here = node(lo)
        carry = (here, quad(lo - 1, before, here))
        if count <= WHOLE:
            run(lo, count, carry)
        else:
            rows = count // 2
            lax.fori_loop(0, 2, lambda i, carry: run(lo + i * rows, rows, carry), carry)

    inv = 1.0 / 0.45

    def forward(start, count):
        p = start // SWEEPS

        def sweep(s, carry):
            def use(k, first, second, u, v):
                c, d = prec[p, k], keep_c[p, k]
                new_u = (d * u + drive_u[p, k]) - c * first
                new_v = (d * v + drive_v[p, k]) - c * second
                fields[0, k] = new_u
                fields[1, k] = new_v
                moments[s, 0, k] = inv * new_u + (1.0 - inv) * u
                moments[s, 1, k] = inv * new_v + (1.0 - inv) * v

            stencil(lambda k: (fields[0, k], fields[1, k]), p, start + 1, EX - 2 - 2 * start, use)
            return carry

        lax.fori_loop(start, start + count, sweep, 0)

    for start, count in FORWARD[:4]:
        forward(start, count)

    everyone = pl.ds(0, n_tile - 1)
    pltpu.make_async_remote_copy(
        src_ref=outgoing.at[everyone, pl.ds(0, n_grp)], dst_ref=first_r.at[everyone, pl.ds(0, n_grp)], send_sem=row_send, recv_sem=row_recv,
        device_id=(g, t), device_id_type=MESH,
    ).wait()
    own = outgoing[t]
    first_r[t] = own
    flat_r = first_r.reshape(n_tile * 8, LANES)
    for k in range(n_grp):
        second_s[k] = flat_r[pl.ds(k, n_tile, stride=8), :]
    second_r[g] = second_s[g]

    def group_copy(step):
        to = lax.rem(g + step, n_grp)
        return pltpu.make_async_remote_copy(
            src_ref=second_s.at[to], dst_ref=second_r.at[g], send_sem=grp_send.at[step - 1],
            recv_sem=grp_recv.at[step - 1], device_id=(to, t), device_id_type=MESH,
        )

    for step in range(1, n_grp):
        group_copy(step).start()

    for start, count in FORWARD[4:SWEEPS]:
        forward(start, count)
    arrive(late)
    settle(5)
    coefficients(1)
    for start, count in FORWARD[SWEEPS:12]:
        forward(start, count)

    for step in range(1, n_grp):
        group_copy(step).wait()
    sources = n_grp * n_tile
    arrived = jnp.transpose(second_r[...].reshape(sources, LANES))
    for s in range(SLOTS):
        spot = arrived[s : s + 1, :].astype(I32)
        at = pl.ds(s * sources, sources)
        gram_b[:, at] = jnp.where(iota((CY, sources), 0) == spot % CY, 1.0, 0.0).astype(BF16)
        chosen = iota((CX, sources), 0) == spot // CY
        for j in range(5):
            row = SLOTS * (j + 1) + s
            value = jnp.where(chosen, arrived[row : row + 1, :], 0.0)
            for q, piece in enumerate(pieces(value)):
                gram_a[pl.ds((q * 5 + j) * CX, CX), at] = piece
    product = lax.dot_general(
        gram_a[...], gram_b[...], (((1,), (1,)), ((), ())), preferred_element_type=F32
    )
    part = 5 * CX
    gram[...] = product[:part] + product[part : 2 * part] + product[2 * part :]

    for start, count in FORWARD[12:]:
        forward(start, count)

    def collect(source, base, r, m):
        a = source[pl.ds(base * SEG + 8 * SEG * r + 2 * m, 8, stride=SEG), :]
        b = source[pl.ds(base * SEG + 8 * SEG * r + 2 * m + 1, 8, stride=SEG), :]
        return jnp.where(lane8 < 64, roll(a, -32), roll(b, 32))

    scale = 1.0 / 16.0

    def misfit_adjoint(r, m):
        u = collect(fields2, W, r, m)
        v = collect(fields2, EX + W, r, m)
        rows, at = pl.ds(8 * r, 8), pl.ds(LANES * m, LANES)
        sxx, sxy, syy, sxo, syo = [gram[pl.ds(j * CX + 8 * r, 8), at] for j in range(5)]
        adj_n[0, rows, at] = scale * (sxx * u + sxy * v - sxo)
        adj_n[1, rows, at] = scale * (sxy * u + syy * v - syo)

    for r in range(CX // 8):
        misfit_adjoint(r, 0)
        misfit_adjoint(r, CY // LANES - 1)
        rows = pl.ds(8 * r, 8)
        aedge_l[rows, :] = jnp.where(
            lane8 < 16, adj_n[0, rows, pl.ds(0, LANES)], roll(adj_n[1, rows, pl.ds(0, LANES)], 16)
        )
        end = pl.ds(CY - LANES, LANES)
        aedge_r[rows, :] = jnp.where(
            lane8 < 16, roll(adj_n[0, rows, end], 16), roll(adj_n[1, rows, end], 32)
        )
    amoves = neighbours(
        [(rows_of(adj_n), adj_t, adj_b)], aedge_l, aedge_r, ahalo_l, ahalo_r, asend_sem, arecv_sem
    )
    begin(amoves[:-2])
    for r in range(CX // 8):
        for m in range(1, CY // LANES - 1):
            misfit_adjoint(r, m)
    begin(amoves[-2:])
    grads[...] = jnp.zeros_like(grads)
    arrive(amoves)
    adj2 = adj.reshape(2 * EX * SEG, LANES)
    for f in range(2):
        for r in range(EX // 8):
            if r < W // 8:
                source, k = adj_t, r
            elif r >= (W + CX) // 8:
                source, k = adj_b, r - (W + CX) // 8
            else:
                source, k = adj_n, r - W // 8
            tiles = [source[f, pl.ds(8 * k, 8), pl.ds(LANES * m, LANES)] for m in range(4)]
            at = pl.ds(8 * r, 8)
            spread(
                adj2, f * EX, 8 * r, tiles,
                roll(ahalo_l[at, :], 16 - 16 * f), roll(ahalo_r[at, :], 96 - 16 * f),
            )

    def gather(position, k, a, b):
        grads[0, k] = grads[0, k] + a
        grads[1, k] = grads[1, k] + b
        grads[2, k] = grads[2, k] - (a * moments[position, 0, k] + b * moments[position, 1, k])

    def backward(start, count):
        p = (STEPS - 1 - start) // SWEEPS

        def sweep(s, carry):
            def load(k):
                c = prec[p, k]
                a, b = c * adj[0, k], c * adj[1, k]
                gather(STEPS - 1 - s, k, a, b)
                return a, b

            def use(k, first, second, a, b):
                d = keep_c[p, k]
                adj[0, k] = d * adj[0, k] - first
                adj[1, k] = d * adj[1, k] - second

            stencil(load, p, start + 2, EX - 4 - 2 * start, use)
            return carry

        lax.fori_loop(start, start + count, sweep, 0)

    for start, count in BACKWARD:
        backward(start, count)
    for k in range(W, W + CX):
        c = prec[0, k]
        gather(0, k, c * adj[0, k], c * adj[1, k])

    grads2 = grads.reshape(3 * EX * SEG, LANES)
    for r in range(CX // 8):
        for m in range(CY // LANES):
            rows, at = pl.ds(8 * r, 8), pl.ds(LANES * m, LANES)
            grad_n[rows, at] = fric[rows, at] * collect(grads2, 2 * EX + W, r, m)

    bins = jnp.zeros((3 * n_tile, LANES), F32)
    for r in range(CX):
        high = (elem[pl.ds(r, 1), :] - first_element) // LANES
        chosen = iota((n_tile, CY), 0) == high
        value = jnp.where(chosen, grad_n[pl.ds(r, 1), :], 0.0)
        bins = bins + lax.dot_general(
            jnp.concatenate(pieces(value), axis=0), one_lo[r], (((1,), (1,)), ((), ())),
            preferred_element_type=F32,
        )
    bins = bins[:n_tile] + bins[n_tile : 2 * n_tile] + bins[2 * n_tile :]
    for k in range(n_tile):
        elem_s[k] = bins[k : k + 1, :]

    for hop in HOPS:
        to = partner(hop)
        pltpu.make_async_remote_copy(
            src_ref=elem_s.at[to], dst_ref=elem_r.at[t], send_sem=el_send, recv_sem=el_recv,
            device_id=(g, to), device_id_type=MESH,
        ).start()
    elem_r[t] = elem_s[t]
    for r in range(CX // 8):
        for m in range(CY // LANES):
            rows, at = pl.ds(8 * r, 8), pl.ds(LANES * m, LANES)
            stress_out[0, rows, at] = collect(grads2, W, r, m)
            stress_out[1, rows, at] = collect(grads2, EX + W, r, m)
    pltpu.make_async_remote_copy(
        src_ref=elem_s.at[everyone], dst_ref=elem_r.at[everyone], send_sem=el_send, recv_sem=el_recv,
        device_id=(g, t), device_id_type=MESH,
    ).wait()
    result = elem_r[0]
    for k in range(1, n_tile):
        result = result + elem_r[k]
    elem_out[...] = result.reshape(LANES)
    leave(moves)
    leave(late)
    leave(amoves)


def shards(vel, stress, visc, fric, elem, observed, look, row_owner, row_cell):
    n_grp, n_tile = lax.axis_size("grp"), lax.axis_size("tile")
    rows = observed.shape[0]
    vmem = pl.BlockSpec(memory_space=pltpu.VMEM)
    hbm = pl.BlockSpec(memory_space=pltpu.HBM)
    coefficient = pltpu.VMEM((PICARD, EX, SEG, LANES), F32)
    edge, side = pltpu.VMEM((CX, LANES), F32), pltpu.VMEM((EX, LANES), F32)
    dma = pltpu.SemaphoreType.DMA
    sources = n_grp * n_tile
    stress_adjoint, elements = pl.pallas_call(
        functools.partial(main_kernel, n_grp, n_tile),
        out_shape=(
            jax.ShapeDtypeStruct((2, CX, CY), F32),
            jax.ShapeDtypeStruct((LANES,), F32),
        ),
        in_specs=[hbm] * 9,
        out_specs=(vmem, vmem),
        scratch_shapes=[
            pltpu.VMEM((2, CX, CY), F32), pltpu.VMEM((2, CX, CY), F32), pltpu.VMEM((2, CX, CY), F32),
            pltpu.VMEM((CX, CY), F32), pltpu.VMEM((CX, CY), I32),
            pltpu.VMEM(observed.shape, F32), pltpu.VMEM(look.shape, F32),
            pltpu.VMEM((1, rows), I32), pltpu.VMEM((1, rows), I32),
            pltpu.VMEM((n_tile, 8, LANES), F32),
            edge, edge,
            pltpu.VMEM((NF, W, CY), F32), pltpu.VMEM((NF, W, CY), F32),
            side, side,
            pltpu.VMEM((2, CX, CY), F32), pltpu.VMEM((2, W, CY), F32), pltpu.VMEM((2, W, CY), F32),
            edge, edge, side, side,
            pltpu.VMEM((n_tile, 8, LANES), F32),
            pltpu.VMEM((n_grp, n_tile, LANES), F32), pltpu.VMEM((n_grp, n_tile, LANES), F32),
            pltpu.VMEM((15 * CX, SLOTS * sources), BF16), pltpu.VMEM((CY, SLOTS * sources), BF16),
            pltpu.VMEM((5 * CX, CY), F32),
            pltpu.VMEM((NF, EX, SEG, LANES), F32),
            coefficient, coefficient, coefficient, coefficient, coefficient, coefficient,
            pltpu.VMEM((STEPS, 2, EX, SEG, LANES), F32),
            pltpu.VMEM((2, EX, SEG, LANES), F32),
            pltpu.VMEM((3, EX, SEG, LANES), F32),
            pltpu.VMEM((CX, CY), F32),
            pltpu.VMEM((CX, LANES, CY), BF16),
            pltpu.VMEM((n_tile, 1, LANES), F32), pltpu.VMEM((n_tile, 1, LANES), F32),
            dma((9,)), dma((16,)), dma((16,)), dma((8,)), dma((8,)),
            dma, dma, dma((n_grp - 1,)), dma((n_grp - 1,)), dma, dma,
        ],
        compiler_params=pltpu.CompilerParams(
            collective_id=0, has_side_effects=True, vmem_limit_bytes=56 << 20
        ),
        name="adjoint",
    )(
        vel, stress, visc, fric, elem, observed, look,
        row_owner.reshape(1, rows), row_cell.reshape(1, rows),
    )
    return stress_adjoint, elements


def solution(mesh):
    both = ("grp", "tile")
    return jax.shard_map(
        shards,
        mesh=mesh,
        in_specs=(
            P(None, "grp", "tile"),
            P(None, "grp", "tile"),
            P(None, "grp", "tile"),
            P("grp", "tile"),
            P("grp", "tile"),
            P(both, None),
            P(None, both, None),
            P(both, None),
            P(both),
        ),
        out_specs=(P(None, "grp", "tile"), P(both)),
        check_vma=False,
    )
```
